32 devices in a mesh: dp: 4 (over y, x), tensor: 8 (over z, core).
Axes of the slice: x: 2, y: 2, z: 4, core: 2. Of those that a mesh axis runs over, the one named last changes fastest.
Arguments:
- tokens: bfloat16 [2048, 8192], P('dp', 'tensor'), may hold values from -6 to 6
- cotangent: bfloat16 [2048, 8192], P('dp', 'tensor'), may hold values from -6 to 6
- w_first: bfloat16 [32, 256, 1024], P('tensor'), may hold values from -0.375 to 0.375
- w_second: bfloat16 [128, 256, 256], P('tensor'), may hold values from -0.375 to 0.375
- third_weight_blocks: bfloat16 [128, 256, 256], P('tensor'), may hold values from -0.375 to 0.375
- w_fourth: bfloat16 [32, 1024, 256], P('tensor'), may hold values from -0.1875 to 0.1875
Outputs:
- layer_out: bfloat16 [2048, 8192], P('dp', 'tensor')
- tokens_grad: bfloat16 [2048, 8192], P('dp', 'tensor')
- grad_first: float32 [32, 256, 1024], P('tensor')
- grad_second: float32 [128, 256, 256], P('tensor')
- grad_third: float32 [128, 256, 256], P('tensor')
- grad_fourth: float32 [32, 1024, 256], P('tensor')
The draws below stay inside these ranges and needn't reach their ends.
All inputs are finite; a program needn't handle non-finite values.
Results may differ from the reference program's by a relative error of at most 0.0095.
Values may be sent and summed in bfloat16 or wider, within the bound.
No kernel may reach another device: no remote copies, remote signals or barrier semaphores. Data moves between devices by JAX's collectives and lax.ppermute only.
A program may use at most 128 MiB of HBM per device.

```python
import math
import jax
import jax.numpy as jnp
from jax import lax

D = 8192
FF = 32768
BLK = 256
NIN = 32
NHID = 128
TOKENS = 2048


def levels(own_key, extent, cuts, least, largest):
    factor_of = 1.0
    for position, parts in cuts:
        steps = jax.random.uniform(jax.random.fold_in(jax.random.fold_in(own_key, 6), position), (parts,), jnp.float32, least / len(cuts), largest / len(cuts))
        factor_of = factor_of * jnp.repeat(jnp.exp(steps), extent[position] // parts).reshape((-1,) + (1,) * (len(extent) - 1 - position))
    return factor_of


def scatter_about(rng, shape, width, reach, shards=(), held_as=jnp.bfloat16):
    values = width * jax.random.normal(rng, shape, jnp.float32)
    if shards:
        values = values * levels(rng, shape, shards, -0.22, 0.18)
    return jnp.clip(values, -reach, reach).astype(held_as)


def setup_inputs(seed: int = 0) -> dict:
    keys = jax.random.split(jax.random.key(seed), 7)
    tokens = scatter_about(keys[0], (TOKENS, D), 1.0, 6.0, ((0, 4), (1, 8)))
    cotangent = scatter_about(keys[1], (TOKENS, D), 1.0, 6.0, ((0, 4), (1, 8)))
    w_first = scatter_about(keys[2], (NIN, BLK, FF // NIN), BLK ** -0.5, 0.375, ((0, 8),))
    w_second = scatter_about(keys[3], (NHID, BLK, BLK), BLK ** -0.5, 0.375, ((0, 8),))
    third_weight_blocks = scatter_about(keys[4], (NHID, BLK, BLK), BLK ** -0.5, 0.375, ((0, 8),))
    w_fourth = scatter_about(keys[5], (NIN, FF // NIN, BLK), (FF // NIN) ** -0.5, 0.1875, ((0, 8),))
    return {"tokens": tokens, "cotangent": cotangent, "w_first": w_first, "w_second": w_second, "third_weight_blocks": third_weight_blocks, "w_fourth": w_fourth}


def gelu_parts(value_in):
    cdf_part = 0.5 * (1.0 + lax.erf(value_in * 0.7071067811865476))
    slope_part = cdf_part + value_in * jnp.exp(-0.5 * value_in * value_in) * 0.3989422804014327
    return (value_in * cdf_part, slope_part)

def reference(tokens, cotangent, w_first, w_second, third_weight_blocks, w_fourth):
    in_blocks = D // BLK
    hid_blocks = FF // BLK
    sub_width = BLK // in_blocks
    tok_block = math.gcd(TOKENS, 512)
    block_count = TOKENS // tok_block
    first_f = w_first.astype(jnp.float32)
    second_view = w_second.astype(jnp.float32).reshape(hid_blocks, in_blocks, sub_width, BLK)
    third_factor_float = third_weight_blocks.astype(jnp.float32)
    fourth_view = w_fourth.astype(jnp.float32).reshape(in_blocks, hid_blocks, sub_width, BLK)
    input_blocks = tokens.reshape(block_count, tok_block, in_blocks, BLK)
    cot_blocks = cotangent.reshape(block_count, tok_block, in_blocks, BLK)

    def step(carry, pieces):
        acc_one, acc_two, acc_three, acc_four = carry
        inputs_f = pieces[0].astype(jnp.float32)
        cot_f = pieces[1].astype(jnp.float32)
        first_out = jnp.einsum('tai,aik->tak', inputs_f, first_f).astype(jnp.bfloat16)
        first_out = first_out.reshape(tok_block, in_blocks, hid_blocks, sub_width)
        first_f32 = first_out.astype(jnp.float32)
        pre_act = jnp.einsum('tabc,bacj->tbj', first_f32, second_view)
        gelu_val, gelu_slope = gelu_parts(pre_act)
        activated = gelu_val.astype(jnp.bfloat16)
        activation_float32 = activated.astype(jnp.float32)
        third_factor_output = jnp.einsum('nul,ulk->nuk', activation_float32, third_factor_float).astype(jnp.bfloat16)
        third_f32 = third_factor_output.astype(jnp.float32).reshape(tok_block, hid_blocks, in_blocks, sub_width)
        out_block = jnp.einsum('tbac,abck->tak', third_f32, fourth_view).astype(jnp.bfloat16)
        third_grad = jnp.einsum('tak,abck->tbac', cot_f, fourth_view).astype(jnp.bfloat16)
        delta_four = jnp.einsum('tbac,tak->abck', third_f32, cot_f)
        third_gradient_matrix = third_grad.astype(jnp.float32).reshape(tok_block, hid_blocks, BLK)
        activation_gradient = jnp.einsum('yhp,hqp->yhq', third_gradient_matrix, third_factor_float)
        pre_grad = (activation_gradient * gelu_slope).astype(jnp.bfloat16)
        third_delta_term = jnp.einsum('osx,osn->sxn', activation_float32, third_gradient_matrix)
        pre_grad_f = pre_grad.astype(jnp.float32)
        first_grad = jnp.einsum('tbj,bacj->tabc', pre_grad_f, second_view).astype(jnp.bfloat16)
        delta_two = jnp.einsum('tabc,tbj->bacj', first_f32, pre_grad_f)
        first_grad_f = first_grad.astype(jnp.float32).reshape(tok_block, in_blocks, hid_blocks * sub_width)
        input_grad = jnp.einsum('tak,aik->tai', first_grad_f, first_f).astype(jnp.bfloat16)
        delta_one = jnp.einsum('tai,tak->aik', inputs_f, first_grad_f)
        new_carry = (acc_one + delta_one, acc_two + delta_two, acc_three + third_delta_term, acc_four + delta_four)
        return (new_carry, (out_block, input_grad))
    init = (jnp.zeros((in_blocks, BLK, hid_blocks * sub_width), jnp.float32), jnp.zeros((hid_blocks, in_blocks, sub_width, BLK), jnp.float32), jnp.zeros((hid_blocks, BLK, BLK), jnp.float32), jnp.zeros((in_blocks, hid_blocks, sub_width, BLK), jnp.float32))
    sums, outputs = lax.scan(step, init, (input_blocks, cot_blocks))
    grad_scale = 1.0 / math.sqrt(TOKENS)
    layer_out = outputs[0].reshape(TOKENS, D)
    tokens_grad = outputs[1].reshape(TOKENS, D)
    grad_first = sums[0] * grad_scale
    grad_second = sums[1].reshape(hid_blocks, BLK, BLK) * grad_scale
    grad_third = sums[2] * grad_scale
    grad_fourth = sums[3].reshape(in_blocks, hid_blocks * sub_width, BLK) * grad_scale
    return (layer_out, tokens_grad, grad_first, grad_second, grad_third, grad_fourth)
```

```python
import functools
import math

import jax
import jax.numpy as jnp
from jax import lax
from jax.experimental import pallas as pl
from jax.experimental.pallas import tpu as pltpu
from jax.sharding import PartitionSpec as P

F32 = jnp.float32
BF16 = jnp.bfloat16


def gelu_parts(value_in):
    cdf_part = 0.5 * (1.0 + lax.erf(value_in * 0.7071067811865476))
    slope_part = cdf_part + value_in * jnp.exp(-0.5 * value_in * value_in) * 0.3989422804014327
    return (value_in * cdf_part, slope_part)


def dot(a, b, ca, cb):
    return lax.dot_general(a, b, (((ca,), (cb,)), ((), ())), preferred_element_type=F32)


def split_rows(val, hid, sub):
    return val.reshape(hid, sub, val.shape[-1])


def expand_kernel(rel_ref, x_ref, w_ref, y_ref, *, wd, bw, hd, sub):
    outs = []
    for a in range(wd):
        val = dot(w_ref[0, a], x_ref[0, a * bw : (a + 1) * bw, :], 1, 0)
        outs.append(val.reshape(hd, sub, val.shape[-1]))
    for a in range(0, wd, 2):
        if a + 1 < wd:
            both = jnp.concatenate(outs[a : a + 2], axis=1)
            y_ref[:, a * sub : (a + 2) * sub, :] = both.astype(BF16)
        else:
            y_ref[:, a * sub : (a + 1) * sub, :] = outs[a].astype(BF16)


def expand(rel, x_rel, w_own, wd, bw, hd, sub):
    n, _, rows = x_rel.shape
    m = w_own.shape[2]
    return pl.pallas_call(
        functools.partial(expand_kernel, wd=wd, bw=bw, hd=hd, sub=sub),
        grid_spec=pltpu.PrefetchScalarGridSpec(
            num_scalar_prefetch=1,
            grid=(n,),
            in_specs=[
                pl.BlockSpec((1, wd * bw, rows), lambda d, rel: (rel[d], 0, 0)),
                pl.BlockSpec((1, wd, m, bw), lambda d, rel: (d, 0, 0, 0)),
            ],
            out_specs=pl.BlockSpec((hd, wd * sub, rows), lambda d, rel: (0, d, 0)),
        ),
        out_shape=jax.ShapeDtypeStruct((hd, n * wd * sub, rows), BF16),
        compiler_params=pltpu.CompilerParams(dimension_semantics=("arbitrary",)),
        cost_estimate=pl.CostEstimate(
            flops=2 * n * wd * m * bw * rows,
            bytes_accessed=2 * (n * wd * bw * rows + n * wd * m * bw + n * wd * m * rows),
            transcendentals=0,
        ),
        name="expand",
    )(rel, x_rel, w_own)


def middle_kernel(y_ref, dz_ref, w2_ref, w3_ref, z_ref, dy_ref, g2_ref, g3_ref, *, scale):
    yb = y_ref[0]
    dzb = dz_ref[0]
    w2 = w2_ref[0]
    w3 = w3_ref[0]
    pre = dot(w2, yb, 0, 0)
    val, slope = gelu_parts(pre)
    act = val.astype(BF16)
    z_ref[0] = dot(w3, act, 0, 0).astype(BF16)
    dact = dot(w3, dzb, 1, 0)
    dpre = (dact * slope).astype(BF16)
    dy_ref[0] = dot(w2, dpre, 1, 0).astype(BF16)
    g2_ref[0] = (dot(yb, dpre, 1, 1) * scale).astype(BF16)
    g3_ref[0] = (dot(act, dzb, 1, 1) * scale).astype(BF16)


def middle(y, dz, w2, w3, scale):
    hd, k, rows = y.shape
    j = w2.shape[2]
    row_spec = pl.BlockSpec((1, k, rows), lambda b: (b, 0, 0))
    w2_spec = pl.BlockSpec((1, k, j), lambda b: (b, 0, 0))
    w3_spec = pl.BlockSpec((1, j, k), lambda b: (b, 0, 0))
    return pl.pallas_call(
        functools.partial(middle_kernel, scale=scale),
        grid=(hd,),
        in_specs=[row_spec, row_spec, w2_spec, w3_spec],
        out_specs=[row_spec, row_spec, w2_spec, w3_spec],
        out_shape=[
            jax.ShapeDtypeStruct(y.shape, BF16),
            jax.ShapeDtypeStruct(y.shape, BF16),
            jax.ShapeDtypeStruct(w2.shape, BF16),
            jax.ShapeDtypeStruct(w3.shape, BF16),
        ],
        compiler_params=pltpu.CompilerParams(dimension_semantics=("arbitrary",)),
        cost_estimate=pl.CostEstimate(
            flops=2 * 6 * hd * k * j * rows,
            bytes_accessed=2 * (4 * hd * k * rows + 4 * hd * k * j),
            transcendentals=2 * hd * j * rows,
        ),
        name="middle",
    )(y, dz, w2, w3)


def contract_kernel(
    rel_ref, dst_ref, z_ref, dy_ref, x_ref, g_ref, w1_ref, w4_ref, out_ref, tg_ref, gr_ref,
    *, wd, bw, hd, sub, dp, scale
):
    rows = z_ref.shape[-1]
    m = hd * sub
    step = m // dp

    def parts(ref):
        vals = []
        for a in range(0, wd, 2):
            width = min(2, wd - a)
            chunk = ref[:, a * sub : (a + width) * sub, :].astype(F32)
            for k in range(width):
                piece = chunk[:, k * sub : (k + 1) * sub, :]
                vals.append(piece.reshape(m, rows).astype(BF16))
        return vals

    zs = parts(z_ref)
    dys = parts(dy_ref)
    for a in range(wd):
        span = slice(a * bw, (a + 1) * bw)
        out_ref[0, span, :] = dot(w4_ref[0, a], zs[a], 0, 0).astype(BF16)
        tg_ref[0, span, :] = dot(w1_ref[0, a], dys[a], 0, 0).astype(BF16)
        g1 = (dot(dys[a], x_ref[0, span, :], 1, 1) * scale).astype(BF16)
        g4 = (dot(zs[a], g_ref[0, span, :], 1, 1) * scale).astype(BF16)
        for q in range(dp):
            gr_ref[q, 0, 0, a] = g1[q * step : (q + 1) * step]
            gr_ref[q, 0, 1, a] = g4[q * step : (q + 1) * step]


def contract(rel, dst, z, dy, x_rel, g_rel, w1t, w4, wd, bw, hd, sub, dp, scale):
    n, _, rows = x_rel.shape
    m = hd * sub
    zspec = pl.BlockSpec((hd, wd * sub, rows), lambda s, rel, dst: (0, dst[s], 0))
    xspec = pl.BlockSpec((1, wd * bw, rows), lambda s, rel, dst: (rel[s], 0, 0))
    wspec = pl.BlockSpec((1, wd, m, bw), lambda s, rel, dst: (dst[s], 0, 0, 0))
    return pl.pallas_call(
        functools.partial(
            contract_kernel, wd=wd, bw=bw, hd=hd, sub=sub, dp=dp, scale=scale
        ),
        grid_spec=pltpu.PrefetchScalarGridSpec(
            num_scalar_prefetch=2,
            grid=(n,),
            in_specs=[zspec, zspec, xspec, xspec, wspec, wspec],
            out_specs=[
                xspec,
                xspec,
                pl.BlockSpec(
                    (dp, 1, 2, wd, m // dp, bw), lambda s, rel, dst: (0, dst[s], 0, 0, 0, 0)
                ),
            ],
        ),
        out_shape=[
            jax.ShapeDtypeStruct(x_rel.shape, BF16),
            jax.ShapeDtypeStruct(x_rel.shape, BF16),
            jax.ShapeDtypeStruct((dp, n, 2, wd, m // dp, bw), BF16),
        ],
        compiler_params=pltpu.CompilerParams(dimension_semantics=("arbitrary",)),
        cost_estimate=pl.CostEstimate(
            flops=2 * 4 * n * wd * m * bw * rows,
            bytes_accessed=2 * (4 * n * wd * bw * rows + 2 * n * wd * m * rows + 4 * n * wd * m * bw),
            transcendentals=0,
        ),
        name="contract",
    )(rel, dst, z, dy, x_rel, g_rel, w1t, w4)


def up_pairs(lo, hi):
    return [(2 * p + c, 2 * p + 2 + c) for p in range(lo, hi) for c in range(2)]


def down_pairs(lo, hi):
    return [(2 * p + 2 + c, 2 * p + c) for p in range(lo, hi) for c in range(2)]


def line_gather(own, nl):
    ups, downs = [own], [own]
    for r in range(1, nl):
        ups.append(lax.ppermute(ups[-1], "tensor", up_pairs(r - 1, nl - 1)))
        downs.append(lax.ppermute(downs[-1], "tensor", down_pairs(0, nl - r)))
    return [own] + [downs[k] + ups[nl - k] for k in range(1, nl)]


def swap(val, n):
    return lax.ppermute(val, "tensor", [(i, i ^ 1) for i in range(n)])


def line_scatter(parts, nl):
    up, down = parts[nl - 1], parts[1]
    for r in range(1, nl):
        up = lax.ppermute(up, "tensor", up_pairs(0, r))
        down = lax.ppermute(down, "tensor", down_pairs(nl - 1 - r, nl - 1))
        if r < nl - 1:
            up = up + parts[nl - 1 - r]
            down = down + parts[r + 1]
    return (parts[0].astype(F32) + up.astype(F32) + down.astype(F32)).astype(BF16)


def gather_all(own, n):
    nl = n // 2
    mine = line_gather(own, nl)
    return jnp.stack([v for p in mine for v in (p, swap(p, n))])


def scatter_all(partial, n):
    nl = n // 2
    parts = []
    for k in range(nl):
        parts.append(partial[2 * k] + swap(partial[2 * k + 1], n))
    return line_scatter(parts, nl)


def body(tokens, cotangent, w_first, w_second, w_third, w_fourth):
    rows = tokens.shape[0]
    wd, bw, _ = w_first.shape
    hd = w_second.shape[0]
    n = lax.axis_size("tensor")
    dp = lax.axis_size("dp")
    nl = n // 2
    sub = bw // (wd * n)
    m = hd * sub
    step = m // dp
    scale = 1.0 / math.sqrt(rows * dp)
    me = lax.axis_index("tensor")
    quarter = lax.axis_index("dp")
    pos, core = me // 2, me % 2

    order = jnp.arange(n, dtype=jnp.int32)
    rel_of = 2 * ((order // 2 - pos + nl) % nl) + (order % 2 + core) % 2
    dst_of = 2 * ((order // 2 + pos) % nl) + (order % 2 + core) % 2

    w14 = jnp.stack([jnp.swapaxes(w_first, 1, 2), w_fourth])
    w14 = w14.reshape(2, wd, n, dp, step, bw)
    w14 = lax.dynamic_index_in_dim(w14, quarter, axis=3, keepdims=False)
    w14 = jnp.transpose(w14, (2, 0, 1, 3, 4))
    w14 = lax.all_to_all(w14, "tensor", split_axis=0, concat_axis=0, tiled=True)
    w14 = lax.all_gather(w14, "dp")
    w14 = jnp.transpose(w14, (2, 1, 3, 0, 4, 5)).reshape(2, n, wd, m, bw)
    w1t, w4 = w14[0], w14[1]

    x_rel = gather_all(tokens.T, n)
    g_rel = gather_all(cotangent.T, n)
    y = expand(rel_of, x_rel, w1t, wd, bw, hd, sub)
    dz = expand(rel_of, g_rel, w4, wd, bw, hd, sub)
    z, dy, g2, g3 = middle(y, dz, w_second, w_third, scale)
    out_part, tg_part, g14 = contract(
        order, dst_of, z, dy, x_rel, g_rel, w1t, w4, wd, bw, hd, sub, dp, scale
    )

    layer_out = scatter_all(out_part, n).T
    tokens_grad = scatter_all(tg_part, n).T

    g2, g3 = lax.psum((g2, g3), "dp")
    g14 = lax.psum_scatter(g14, "dp")
    g14 = lax.all_to_all(g14, "tensor", split_axis=0, concat_axis=0, tiled=True)
    g14 = lax.all_gather(g14, "dp")
    g1 = jnp.transpose(g14[:, :, 0], (2, 4, 1, 0, 3)).reshape(wd, bw, n * m).astype(F32)
    g4 = jnp.transpose(g14[:, :, 1], (2, 1, 0, 3, 4)).reshape(wd, n * m, bw).astype(F32)
    return (layer_out, tokens_grad, g1, g2.astype(F32), g3.astype(F32), g4)


def solution(mesh):
    return jax.shard_map(
        body,
        mesh=mesh,
        in_specs=(
            P("dp", "tensor"),
            P("dp", "tensor"),
            P("tensor", None, None),
            P("tensor", None, None),
            P("tensor", None, None),
            P("tensor", None, None),
        ),
        out_specs=(
            P("dp", "tensor"),
            P("dp", "tensor"),
            P("tensor", None, None),
            P("tensor", None, None),
            P("tensor", None, None),
            P("tensor", None, None),
        ),
        check_vma=False,
    )
```

```python
import functools
import math

import jax
import jax.numpy as jnp
from jax import lax
from jax.experimental import pallas as pl
from jax.experimental.pallas import tpu as pltpu
from jax.sharding import PartitionSpec as P

F32 = jnp.float32
BF16 = jnp.bfloat16
PARAMS = pltpu.CompilerParams(dimension_semantics=("arbitrary",))


def gelu_parts(value_in):
    cdf_part = 0.5 * (1.0 + lax.erf(value_in * 0.7071067811865476))
    slope_part = cdf_part + value_in * jnp.exp(-0.5 * value_in * value_in) * 0.3989422804014327
    return (value_in * cdf_part, slope_part)


def dot(a, b, ca, cb):
    return lax.dot_general(a, b, (((ca,), (cb,)), ((), ())), preferred_element_type=F32)


def cost(flops, elements, trans=0):
    return pl.CostEstimate(flops=flops, bytes_accessed=2 * elements, transcendentals=trans)


def expand_kernel(meta, x_ref, w_ref, own_ref, send_ref, *, pa, bw, hd, sub):
    low = meta[1] == 0
    m = hd * sub
    for e in range(2):
        own, send = [], []
        for a in range(pa):
            val = dot(w_ref[e, 0, a], x_ref[e, a * bw : (a + 1) * bw, :], 1, 0)
            first = val[:m].reshape(hd, sub, val.shape[-1])
            second = val[m:].reshape(hd, sub, val.shape[-1])
            own.append(jnp.where(low, first, second))
            send.append(jnp.where(low, second, first))
        own_ref[e] = jnp.concatenate(own, axis=1).astype(BF16)
        send_ref[e] = jnp.concatenate(send, axis=1).astype(BF16)


def expand(meta, xg, w14, hd, sub):
    _, nl, wd, m2, bw = w14.shape
    rows = xg.shape[-1]
    pa = min(wd, 2)
    out = jax.ShapeDtypeStruct((2, hd, wd * sub, rows), BF16)
    out_spec = pl.BlockSpec((2, hd, pa * sub, rows), lambda s, meta: (0, 0, s, 0))
    return pl.pallas_call(
        functools.partial(expand_kernel, pa=pa, bw=bw, hd=hd, sub=sub),
        grid_spec=pltpu.PrefetchScalarGridSpec(
            num_scalar_prefetch=1,
            grid=(wd // pa,),
            in_specs=[
                pl.BlockSpec((2, pa * bw, rows), lambda s, meta: (0, s, 0)),
                pl.BlockSpec((2, 1, pa, m2, bw), lambda s, meta: (0, meta[0], s, 0, 0)),
            ],
            out_specs=[out_spec, out_spec],
        ),
        out_shape=[out, out],
        compiler_params=PARAMS,
        cost_estimate=cost(4 * wd * m2 * bw * rows, 2 * wd * (bw * rows + m2 * bw + m2 * rows)),
        name="expand",
    )(meta, xg, w14)


def middle_kernel(meta, *refs, nl, part, dp, scale):
    slots = nl + 1
    owns, recvs = refs[:slots], refs[slots : 2 * slots]
    w2_ref, w3_ref, own_ref, send_ref, g2_ref, g3_ref, ysc = refs[2 * slots :]
    pos, core = meta[0], meta[1]

    def place(k, where):
        base = pl.multiple_of((where * 2 + core) * part, part)
        other = pl.multiple_of((where * 2 + 1 - core) * part, part)
        for e in range(2):
            ysc[e, pl.ds(base, part), :] = owns[k][e, 0].astype(F32)
            ysc[e, pl.ds(other, part), :] = recvs[k][e, 0].astype(F32)

    for k in range(nl):
        place(k, lax.rem(pos + k, nl))

    @pl.when(meta[2] >= 0)
    def _():
        place(nl, meta[2])

    yb = ysc[0].astype(BF16)
    dzb = ysc[1].astype(BF16)
    w2 = w2_ref[0]
    w3 = w3_ref[0]
    pre = dot(w2, yb, 0, 0)
    val, slope = gelu_parts(pre)
    act = val.astype(BF16)
    dact = dot(w3, dzb, 1, 0)
    dpre = (dact * slope).astype(BF16)
    g2 = (dot(yb, dpre, 1, 1) * scale).astype(BF16)
    g3 = (dot(act, dzb, 1, 1) * scale).astype(BF16)
    step = g2.shape[0] // dp
    for q in range(dp):
        g2_ref[meta[4 + q], 0] = g2[q * step : (q + 1) * step]
        g3_ref[meta[4 + dp + q], 0] = g3[q * step : (q + 1) * step]
    ysc[0] = dot(w3, act, 0, 0)
    ysc[1] = dot(w2, dpre, 1, 0)
    for k in range(nl):
        for e in range(2):
            base = pl.multiple_of((k * 2 + core) * part, part)
            other = pl.multiple_of((k * 2 + 1 - core) * part, part)
            own_ref[e, 0, k * part : (k + 1) * part] = ysc[e, pl.ds(base, part), :].astype(BF16)
            send_ref[e, 0, k * part : (k + 1) * part] = ysc[e, pl.ds(other, part), :].astype(BF16)


def middle(meta, owns, recvs, w2, w3, dp, scale):
    hd, k, j = w2.shape
    nl = len(owns) - 1
    _, _, part, rows = owns[0].shape
    slot = pl.BlockSpec((2, 1, part, rows), lambda b, meta: (0, b, 0, 0))
    full = pl.BlockSpec((2, 1, nl * part, rows), lambda b, meta: (0, b, 0, 0))
    wspec = pl.BlockSpec((1, k, j), lambda b, meta: (b, 0, 0))
    gspec = pl.BlockSpec((dp, 1, k // dp, j), lambda b, meta: (0, b, 0, 0))
    zout = jax.ShapeDtypeStruct((2, hd, nl * part, rows), BF16)
    gout = jax.ShapeDtypeStruct((dp, hd, k // dp, j), BF16)
    return pl.pallas_call(
        functools.partial(middle_kernel, nl=nl, part=part, dp=dp, scale=scale),
        grid_spec=pltpu.PrefetchScalarGridSpec(
            num_scalar_prefetch=1,
            grid=(hd,),
            in_specs=[slot] * (2 * nl + 2) + [wspec, wspec],
            out_specs=[full, full, gspec, gspec],
            scratch_shapes=[pltpu.VMEM((2, k, rows), F32)],
        ),
        out_shape=[zout, zout, gout, gout],
        compiler_params=PARAMS,
        cost_estimate=cost(
            12 * hd * k * j * rows, 4 * hd * k * rows + 4 * hd * k * j, 2 * hd * j * rows
        ),
        name="middle",
    )(meta, *owns, *recvs, w2, w3)


def contract_kernel(meta, *refs, late, chain, pa, bw, hd, sub, dp, scale):
    refs = list(refs)
    zo_ref, zr_ref, w_ref, x_ref = refs[:4]
    refs = refs[4:]
    late_ref = refs.pop(0) if late else None
    if chain:
        refs = refs[2:]
    part_ref, g1_ref, g4_ref, zsc = refs
    core = meta[1]
    rows = zo_ref.shape[-1]
    m = hd * sub
    step = 2 * m // dp
    mine = pl.multiple_of(core * m, m)
    other = pl.multiple_of((1 - core) * m, m)
    for e in range(2):
        for ref, base in ((zo_ref, mine), (zr_ref, other)):
            chunk = ref[e].astype(F32)
            for a in range(pa):
                piece = chunk[:, a * sub : (a + 1) * sub, :].reshape(m, rows)
                zsc[e, a, pl.ds(base, m), :] = piece.astype(BF16)
    for a in range(pa):
        span = slice(a * bw, (a + 1) * bw)
        z, dy = zsc[0, a], zsc[1, a]
        part_ref[0, span, :] = dot(w_ref[1, 0, a], z, 0, 0).astype(BF16)
        part_ref[1, span, :] = dot(w_ref[0, 0, a], dy, 0, 0).astype(BF16)
        x, g = x_ref[0, span, :], x_ref[1, span, :]
        if late:
            take = meta[3] > 0
            x = jnp.where(take, late_ref[0, span, :], x)
            g = jnp.where(take, late_ref[1, span, :], g)
        g1 = (dot(dy, x, 1, 1) * scale).astype(BF16)
        g4 = (dot(z, g, 1, 1) * scale).astype(BF16)
        for q in range(dp):
            g1_ref[meta[4 + q], 0, a] = g1[q * step : (q + 1) * step]
            g4_ref[meta[4 + dp + q], 0, a] = g4[q * step : (q + 1) * step]


def contract(meta, z_own, z_recv, w14, xg, late, grads, sub, dp, scale):
    _, nl, wd, m2, bw = w14.shape
    hd, rows = z_own.shape[1], z_own.shape[-1]
    pa = min(wd, 2)
    steps = wd // pa
    zspec = pl.BlockSpec((2, hd, pa * sub, rows), lambda s, meta: (0, 0, meta[0] * steps + s, 0))
    xspec = pl.BlockSpec((2, pa * bw, rows), lambda s, meta: (0, s, 0))
    wspec = pl.BlockSpec((2, 1, pa, m2, bw), lambda s, meta: (0, meta[0], s, 0, 0))
    gspec = pl.BlockSpec((dp, 1, pa, m2 // dp, bw), lambda s, meta: (0, meta[0], s, 0, 0))
    gout = jax.ShapeDtypeStruct((dp, nl, wd, m2 // dp, bw), BF16)
    args = [meta, z_own, z_recv, w14, xg]
    specs = [zspec, zspec, wspec, xspec]
    if late is not None:
        args.append(late)
        specs.append(xspec)
    aliases = {}
    if grads is not None:
        aliases = {len(args): 1, len(args) + 1: 2}
        args += list(grads)
        specs += [pl.BlockSpec(memory_space=pl.ANY)] * 2
    return pl.pallas_call(
        functools.partial(
            contract_kernel,
            late=late is not None,
            chain=grads is not None,
            pa=pa,
            bw=bw,
            hd=hd,
            sub=sub,
            dp=dp,
            scale=scale,
        ),
        grid_spec=pltpu.PrefetchScalarGridSpec(
            num_scalar_prefetch=1,
            grid=(steps,),
            in_specs=specs,
            out_specs=[xspec, gspec, gspec],
            scratch_shapes=[pltpu.VMEM((2, pa, m2, rows), BF16)],
        ),
        out_shape=[jax.ShapeDtypeStruct(xg.shape, BF16), gout, gout],
        input_output_aliases=aliases,
        compiler_params=PARAMS,
        cost_estimate=cost(
            8 * wd * m2 * bw * rows, 2 * wd * (2 * bw * rows + m2 * rows + 2 * m2 * bw)
        ),
        name="contract",
    )(*args)


def finish_kernel(tab, p_ref, q_ref, o_ref, *, dp, flip):
    half = dp // 2
    for q in range(dp):
        slot = tab[q]
        inner = lax.rem(slot, half)
        val = jnp.where(slot < half, p_ref[inner, 0, 0].astype(F32), q_ref[inner, 0, 0].astype(F32))
        step = val.shape[0]
        if flip:
            o_ref[0, :, q * step : (q + 1) * step] = val.T
        else:
            o_ref[0, q * step : (q + 1) * step, :] = val


def finish_flip_kernel(tab, p_ref, q_ref, o_ref, *, dp):
    half = dp // 2
    vals = []
    for q in range(dp):
        slot = tab[q]
        inner = lax.rem(slot, half)
        vals.append(
            jnp.where(slot < half, p_ref[inner, 0, 0].astype(F32), q_ref[inner, 0, 0].astype(F32))
        )
    o_ref[0] = jnp.concatenate(vals, axis=0).T


def finish(tab, halves, flip):
    p, q = halves
    half, outer, wd, step, bw = p.shape
    dp = 2 * half
    size = dp * step
    spec = pl.BlockSpec((half, 1, 1, step, bw), lambda o, a, tab: (0, o, a, 0, 0))
    if flip:
        shape, ospec = (wd, bw, outer * size), pl.BlockSpec((1, bw, size), lambda o, a, tab: (a, 0, o))
        body = functools.partial(finish_flip_kernel, dp=dp)
        if size % 128:
            merged = jnp.concatenate([p, q], axis=0)[tab]
            return jnp.transpose(merged, (2, 4, 1, 0, 3)).reshape(shape).astype(F32)
    else:
        shape, ospec = (wd, outer * size, bw), pl.BlockSpec((1, size, bw), lambda o, a, tab: (a, o, 0))
        body = functools.partial(finish_kernel, dp=dp, flip=False)
    return pl.pallas_call(
        body,
        grid_spec=pltpu.PrefetchScalarGridSpec(
            num_scalar_prefetch=1, grid=(outer, wd), in_specs=[spec, spec], out_specs=ospec
        ),
        out_shape=jax.ShapeDtypeStruct(shape, F32),
        compiler_params=pltpu.CompilerParams(dimension_semantics=("arbitrary", "arbitrary")),
        cost_estimate=cost(0, 3 * wd * outer * size * bw),
        name="finish",
    )(tab, p, q)


def up_pairs(lo, hi):
    return [(2 * p + c, 2 * p + 2 + c) for p in range(lo, hi) for c in range(2)]


def down_pairs(lo, hi):
    return [(2 * p + 2 + c, 2 * p + c) for p in range(lo, hi) for c in range(2)]


def swap(val, n):
    return lax.ppermute(val, "tensor", [(i, i ^ 1) for i in range(n)])


def add(a, b):
    return (a.astype(F32) + b.astype(F32)).astype(BF16)


def line_scatter(parts, nl):
    up, down = parts[nl - 1], parts[1]
    for r in range(1, nl):
        up = lax.ppermute(up, "tensor", up_pairs(0, r))
        down = lax.ppermute(down, "tensor", down_pairs(nl - 1 - r, nl - 1))
        if r < nl - 1:
            up = add(up, parts[nl - 1 - r])
            down = add(down, parts[r + 1])
    return (parts[0].astype(F32) + up.astype(F32) + down.astype(F32)).astype(BF16)


X_PAIRS = [(i, i ^ 1) for i in range(4)]
Y_PAIRS = [(i, i ^ 2) for i in range(4)]


def reduce_dp(val, dp, pairs):
    if dp != 4:
        return lax.psum_scatter(val, "dp")
    kept = add(val[:2], lax.ppermute(val[2:], "dp", pairs[0]))
    return add(kept[0], lax.ppermute(kept[1], "dp", pairs[1]))


def gather_dp(val, dp, pairs):
    if dp != 4:
        every = lax.all_gather(val, "dp")
        return every[: dp // 2], every[dp // 2 :]
    low = jnp.stack([val, lax.ppermute(val, "dp", pairs[1])])
    return low, lax.ppermute(low, "dp", pairs[0])


def body(tokens, cotangent, w_first, w_second, w_third, w_fourth):
    rows = tokens.shape[0]
    wd, bw, _ = w_first.shape
    hd = w_second.shape[0]
    n = lax.axis_size("tensor")
    dp = lax.axis_size("dp")
    nl = n // 2
    sub = bw // (wd * n)
    m2 = 2 * hd * sub
    step = m2 // dp
    scale = 1.0 / math.sqrt(rows * dp)
    me = lax.axis_index("tensor")
    mine = lax.axis_index("dp")
    pos, core = me // 2, me % 2
    lines = [[2 * p + c for p in range(nl)] for c in range(2)]
    x_first, y_first = (X_PAIRS, Y_PAIRS), (Y_PAIRS, X_PAIRS)

    dps = jnp.arange(dp, dtype=jnp.int32)
    if dp == 4:
        flips = dps ^ mine
        tab_x = ((flips & 1) << 1) | (flips >> 1)
        tab_y = flips
    else:
        tab_x = tab_y = dps
    low_end, high_end = pos == 0, pos == nl - 1
    late_pos = jnp.where(low_end, nl - 1, jnp.where(high_end, 0, -1))

    def meta_of(head, late):
        head = jnp.stack([jnp.asarray(v, jnp.int32) for v in (head, core, late_pos, late)])
        return jnp.concatenate([head, tab_x, tab_y])

    w14 = jnp.stack([jnp.swapaxes(w_first, 1, 2), w_fourth])
    w14 = w14.reshape(2, wd, nl, dp, step, bw)
    w14 = lax.dynamic_index_in_dim(w14, mine, axis=3, keepdims=False)
    w14 = jnp.transpose(w14, (2, 0, 1, 3, 4))
    w14 = lax.all_to_all(
        w14, "tensor", split_axis=0, concat_axis=0, axis_index_groups=lines, tiled=True
    )
    sides = []
    for e, (pairs, tab) in enumerate(((x_first, tab_x), (y_first, tab_y))):
        every = jnp.concatenate(gather_dp(w14[:, e], dp, pairs))
        every = [lax.dynamic_index_in_dim(every, tab[q], keepdims=False) for q in range(dp)]
        sides.append(jnp.stack(every, axis=2).reshape(nl, wd, m2, bw))
    w14 = jnp.stack(sides)

    own = jnp.stack([tokens.T, cotangent.T])
    ups, downs = [own], [own]
    for r in range(1, nl):
        ups.append(lax.ppermute(ups[-1], "tensor", up_pairs(r - 1, nl - 1)))
        downs.append(lax.ppermute(downs[-1], "tensor", down_pairs(0, nl - r)))
    slots = [own]
    for k in range(1, nl):
        if k == 1:
            slots.append(downs[1])
        elif k == nl - 1:
            slots.append(ups[1])
        else:
            slots.append(downs[k] + ups[nl - k])
    late = ups[nl - 1] + downs[nl - 1]
    metas = [meta_of((pos + k) % nl, 0) for k in range(nl)]
    metas[1] = meta_of((pos + 1) % nl, high_end)
    metas[nl - 1] = meta_of((pos + nl - 1) % nl, low_end)
    late_meta = meta_of(jnp.maximum(late_pos, 0), 0)

    owns, recvs = [], []
    for meta, xg in zip(metas + [late_meta], slots + [late]):
        mine_part, send = expand(meta, xg, w14, hd, sub)
        owns.append(mine_part)
        recvs.append(swap(send, n))
    z_own, z_send, g2, g3 = middle(
        meta_of(pos, 0), owns, recvs, w_second, w_third, dp, scale
    )
    z_recv = swap(z_send, n)

    parts, grads = [None] * nl, None
    order = [k for pair in zip(range(nl - 1, nl // 2, -1), range(1, nl // 2)) for k in pair]
    for k in order + [nl // 2, 0]:
        extra = late if k in (1, nl - 1) else None
        parts[k], g1, g4 = contract(
            metas[k], z_own, z_recv, w14, slots[k], extra, grads, sub, dp, scale
        )
        grads = (g1, g4)
    both = line_scatter(parts, nl)

    g2 = gather_dp(reduce_dp(g2, dp, x_first), dp, x_first)
    g3 = gather_dp(reduce_dp(g3, dp, y_first), dp, y_first)
    g1 = reduce_dp(grads[0], dp, x_first)
    g4 = reduce_dp(grads[1], dp, y_first)
    g14 = jnp.stack([g1, g4], axis=1)
    g14 = lax.all_to_all(
        g14, "tensor", split_axis=0, concat_axis=0, axis_index_groups=lines, tiled=True
    )
    g1 = gather_dp(g14[:, 0], dp, x_first)
    g4 = gather_dp(g14[:, 1], dp, y_first)

    def single(halves):
        return [h[:, None] for h in halves]

    return (
        both[0].T,
        both[1].T,
        finish(tab_x, g1, True),
        finish(tab_x, single(g2), False),
        finish(tab_y, single(g3), False),
        finish(tab_y, g4, False),
    )


def solution(mesh):
    return jax.shard_map(
        body,
        mesh=mesh,
        in_specs=(
            P("dp", "tensor"),
            P("dp", "tensor"),
            P("tensor", None, None),
            P("tensor", None, None),
            P("tensor", None, None),
            P("tensor", None, None),
        ),
        out_specs=(
            P("dp", "tensor"),
            P("dp", "tensor"),
            P("tensor", None, None),
            P("tensor", None, None),
            P("tensor", None, None),
            P("tensor", None, None),
        ),
        check_vma=False,
    )
```

```python
import functools
import math

import jax
import jax.numpy as jnp
from jax import lax
from jax.experimental import pallas as pl
from jax.experimental.pallas import tpu as pltpu
from jax.sharding import PartitionSpec as P

F32 = jnp.float32
BF16 = jnp.bfloat16
PARAMS = pltpu.CompilerParams(dimension_semantics=("arbitrary",))


def gelu_parts(value_in):
    cdf_part = 0.5 * (1.0 + lax.erf(value_in * 0.7071067811865476))
    slope_part = cdf_part + value_in * jnp.exp(-0.5 * value_in * value_in) * 0.3989422804014327
    return (value_in * cdf_part, slope_part)


def dot(a, b, ca, cb):
    return lax.dot_general(a, b, (((ca,), (cb,)), ((), ())), preferred_element_type=F32)


def cost(flops, elements, trans=0):
    return pl.CostEstimate(flops=flops, bytes_accessed=2 * elements, transcendentals=trans)


def expand_kernel(meta, *refs, pa, bw, hd, sub):
    x_refs, (w_ref, own_ref, send_ref) = refs[:-3], refs[-3:]
    low = meta[1] == 0
    m = hd * sub
    for e in range(2):
        own, send = [], []
        for a in range(pa):
            x = total(x_refs, e, slice(a * bw, (a + 1) * bw))
            val = dot(w_ref[e, 0, a], x, 1, 0)
            first = val[:m].reshape(hd, sub, val.shape[-1])
            second = val[m:].reshape(hd, sub, val.shape[-1])
            own.append(jnp.where(low, first, second))
            send.append(jnp.where(low, second, first))
        own_ref[e] = jnp.concatenate(own, axis=1).astype(BF16)
        send_ref[e] = jnp.concatenate(send, axis=1).astype(BF16)


def total(refs, e, span):
    val = refs[0][e, span, :]
    for ref in refs[1:]:
        val = val + ref[e, span, :]
    return val


def expand(meta, xgs, w14, hd, sub):
    _, nl, wd, m2, bw = w14.shape
    rows = xgs[0].shape[-1]
    pa = min(wd, 2)
    out = jax.ShapeDtypeStruct((2, hd, wd * sub, rows), BF16)
    out_spec = pl.BlockSpec((2, hd, pa * sub, rows), lambda s, meta: (0, 0, s, 0))
    return pl.pallas_call(
        functools.partial(expand_kernel, pa=pa, bw=bw, hd=hd, sub=sub),
        grid_spec=pltpu.PrefetchScalarGridSpec(
            num_scalar_prefetch=1,
            grid=(wd // pa,),
            in_specs=[pl.BlockSpec((2, pa * bw, rows), lambda s, meta: (0, s, 0))] * len(xgs)
            + [pl.BlockSpec((2, 1, pa, m2, bw), lambda s, meta: (0, meta[0], s, 0, 0))],
            out_specs=[out_spec, out_spec],
        ),
        out_shape=[out, out],
        compiler_params=PARAMS,
        cost_estimate=cost(4 * wd * m2 * bw * rows, 2 * wd * (bw * rows + m2 * bw + m2 * rows)),
        name="expand",
    )(meta, *xgs, w14)


def put_shares(meta, first, gsc, val, keep_ref, send_ref, index, dp):
    gsc[...] = val
    step = val.shape[0] // dp
    half = dp // 2
    for p in range(dp):
        row = pl.multiple_of(meta[first + p] * step, step)
        ref = keep_ref if p < half else send_ref
        ref[(p % half, *index)] = gsc[pl.ds(row, step), :].astype(BF16)


def middle_kernel(meta, *refs, nl, part, hb, dp, scale):
    slots = nl + 1
    owns, recvs = refs[:slots], refs[slots : 2 * slots]
    (w2_ref, w3_ref, own_ref, send_ref, g2k_ref, g2s_ref, g3k_ref, g3s_ref, ysc, gsc) = refs[2 * slots :]
    pos, core = meta[0], meta[1]

    for b in range(hb):

        def place(k, where):
            base = pl.multiple_of((where * 2 + core) * part, part)
            other = pl.multiple_of((where * 2 + 1 - core) * part, part)
            for e in range(2):
                ysc[b, e, pl.ds(base, part), :] = owns[k][e, b].astype(F32)
                ysc[b, e, pl.ds(other, part), :] = recvs[k][e, b].astype(F32)

        for k in range(nl):
            place(k, lax.rem(pos + k, nl))

        @pl.when(meta[2] >= 0)
        def _():
            place(nl, meta[2])

    for b in range(hb):
        yb = ysc[b, 0].astype(BF16)
        dzb = ysc[b, 1].astype(BF16)
        w2 = w2_ref[b]
        w3 = w3_ref[b]
        pre = dot(w2, yb, 0, 0)
        dact = dot(w3, dzb, 1, 0)
        val, slope = gelu_parts(pre)
        act = val.astype(BF16)
        dpre = (dact * slope).astype(BF16)
        put_shares(meta, 4, gsc.at[b, 0], dot(yb, dpre, 1, 1) * scale, g2k_ref, g2s_ref, (b,), dp)
        put_shares(meta, 4 + dp, gsc.at[b, 1], dot(act, dzb, 1, 1) * scale, g3k_ref, g3s_ref, (b,), dp)
        ysc[b, 0] = dot(w3, act, 0, 0)
        ysc[b, 1] = dot(w2, dpre, 1, 0)
        for k in range(nl):
            for e in range(2):
                base = pl.multiple_of((k * 2 + core) * part, part)
                other = pl.multiple_of((k * 2 + 1 - core) * part, part)
                own_ref[e, b, k * part : (k + 1) * part] = ysc[b, e, pl.ds(base, part), :].astype(BF16)
                send_ref[e, b, k * part : (k + 1) * part] = ysc[b, e, pl.ds(other, part), :].astype(BF16)


def middle(meta, owns, recvs, w2, w3, dp, scale):
    hd, k, j = w2.shape
    nl = len(owns) - 1
    _, _, part, rows = owns[0].shape
    hb = 2
    half = dp // 2
    slot = pl.BlockSpec((2, hb, part, rows), lambda b, meta: (0, b, 0, 0))
    full = pl.BlockSpec((2, hb, nl * part, rows), lambda b, meta: (0, b, 0, 0))
    wspec = pl.BlockSpec((hb, k, j), lambda b, meta: (b, 0, 0))
    gspec = pl.BlockSpec((half, hb, k // dp, j), lambda b, meta: (0, b, 0, 0))
    zout = jax.ShapeDtypeStruct((2, hd, nl * part, rows), BF16)
    gout = jax.ShapeDtypeStruct((half, hd, k // dp, j), BF16)
    return pl.pallas_call(
        functools.partial(middle_kernel, nl=nl, part=part, hb=hb, dp=dp, scale=scale),
        grid_spec=pltpu.PrefetchScalarGridSpec(
            num_scalar_prefetch=1,
            grid=(hd // hb,),
            in_specs=[slot] * (2 * nl + 2) + [wspec, wspec],
            out_specs=[full, full, gspec, gspec, gspec, gspec],
            scratch_shapes=[pltpu.VMEM((hb, 2, k, rows), F32), pltpu.VMEM((hb, 2, k, j), F32)],
        ),
        out_shape=[zout, zout, gout, gout, gout, gout],
        compiler_params=PARAMS,
        cost_estimate=cost(
            12 * hd * k * j * rows, 4 * hd * k * rows + 4 * hd * k * j, 2 * hd * j * rows
        ),
        name="middle",
    )(meta, *owns, *recvs, w2, w3)


def contract_kernel(meta, *refs, nx, late, chain, pa, bw, hd, sub, dp, scale):
    refs = list(refs)
    zo_ref, zr_ref, w_ref = refs[:3]
    x_refs = refs[3 : 3 + nx]
    refs = refs[3 + nx + (4 if chain else 0) :]
    part_ref, g1k_ref, g1s_ref, g4k_ref, g4s_ref, zsc, gsc = refs
    core = meta[1]
    rows = zo_ref.shape[-1]
    m = hd * sub
    mine = pl.multiple_of(core * m, m)
    other = pl.multiple_of((1 - core) * m, m)
    for e in range(2):
        for ref, base in ((zo_ref, mine), (zr_ref, other)):
            chunk = ref[e].astype(F32)
            for a in range(pa):
                piece = chunk[:, a * sub : (a + 1) * sub, :].reshape(m, rows)
                zsc[e, a, pl.ds(base, m), :] = piece.astype(BF16)
    for a in range(pa):
        span = slice(a * bw, (a + 1) * bw)
        z, dy = zsc[0, a], zsc[1, a]
        if late:
            take = meta[3] > 0
            x, g = (jnp.where(take, x_refs[1][e, span, :], x_refs[0][e, span, :]) for e in range(2))
        else:
            x, g = (total(x_refs, e, span) for e in range(2))
        put_shares(meta, 4, gsc.at[a, 0], dot(dy, x, 1, 1) * scale, g1k_ref, g1s_ref, (0, a), dp)
        put_shares(meta, 4 + dp, gsc.at[a, 1], dot(z, g, 1, 1) * scale, g4k_ref, g4s_ref, (0, a), dp)
        part_ref[0, span, :] = dot(w_ref[1, 0, a], z, 0, 0).astype(BF16)
        part_ref[1, span, :] = dot(w_ref[0, 0, a], dy, 0, 0).astype(BF16)


def contract(meta, z_own, z_recv, w14, xgs, late, grads, sub, dp, scale):
    _, nl, wd, m2, bw = w14.shape
    hd, rows = z_own.shape[1], z_own.shape[-1]
    pa = min(wd, 2)
    steps = wd // pa
    half = dp // 2
    zspec = pl.BlockSpec((2, hd, pa * sub, rows), lambda s, meta: (0, 0, meta[0] * steps + s, 0))
    xspec = pl.BlockSpec((2, pa * bw, rows), lambda s, meta: (0, s, 0))
    wspec = pl.BlockSpec((2, 1, pa, m2, bw), lambda s, meta: (0, meta[0], s, 0, 0))
    gspec = pl.BlockSpec((half, 1, pa, m2 // dp, bw), lambda s, meta: (0, meta[0], s, 0, 0))
    gout = jax.ShapeDtypeStruct((half, nl, wd, m2 // dp, bw), BF16)
    args = [meta, z_own, z_recv, w14, *xgs]
    specs = [zspec, zspec, wspec] + [xspec] * len(xgs)
    aliases = {}
    if grads is not None:
        aliases = {len(args) + i: 1 + i for i in range(4)}
        args += list(grads)
        specs += [pl.BlockSpec(memory_space=pl.ANY)] * 4
    return pl.pallas_call(
        functools.partial(
            contract_kernel,
            nx=len(xgs),
            late=late,
            chain=grads is not None,
            pa=pa,
            bw=bw,
            hd=hd,
            sub=sub,
            dp=dp,
            scale=scale,
        ),
        grid_spec=pltpu.PrefetchScalarGridSpec(
            num_scalar_prefetch=1,
            grid=(steps,),
            in_specs=specs,
            out_specs=[xspec, gspec, gspec, gspec, gspec],
            scratch_shapes=[pltpu.VMEM((2, pa, m2, rows), BF16), pltpu.VMEM((pa, 2, m2, bw), F32)],
        ),
        out_shape=[jax.ShapeDtypeStruct(xgs[0].shape, BF16), gout, gout, gout, gout],
        input_output_aliases=aliases,
        compiler_params=PARAMS,
        cost_estimate=cost(
            8 * wd * m2 * bw * rows, 2 * wd * (2 * bw * rows + m2 * rows + 2 * m2 * bw)
        ),
        name="contract",
    )(*args)


def finish_kernel(tab, p_ref, q_ref, o_ref, *, dp, flip):
    half = dp // 2
    count = o_ref.shape[0]
    for a in range(count):
        vals = []
        for q in range(dp):
            slot = tab[q]
            inner = lax.rem(slot, half)
            vals.append(jnp.where(slot < half, p_ref[inner, 0, a], q_ref[inner, 0, a]).astype(F32))
        if flip:
            o_ref[a] = jnp.concatenate(vals, axis=0).T
        else:
            step = vals[0].shape[0]
            for q in range(dp):
                o_ref[a, q * step : (q + 1) * step, :] = vals[q]


def finish(tab, halves, flip):
    p, q = halves
    half, outer, wd, step, bw = p.shape
    dp = 2 * half
    size = dp * step
    count = min(wd, 4)
    spec = pl.BlockSpec((half, 1, count, step, bw), lambda o, a, tab: (0, o, a, 0, 0))
    if flip:
        if size % 128:
            merged = jnp.concatenate([p, q], axis=0)[tab]
            return jnp.transpose(merged, (2, 4, 1, 0, 3)).reshape(wd, bw, outer * size).astype(F32)
        shape = (wd, bw, outer * size)
        ospec = pl.BlockSpec((count, bw, size), lambda o, a, tab: (a, 0, o))
    else:
        shape = (wd, outer * size, bw)
        ospec = pl.BlockSpec((count, size, bw), lambda o, a, tab: (a, o, 0))
    return pl.pallas_call(
        functools.partial(finish_kernel, dp=dp, flip=flip),
        grid_spec=pltpu.PrefetchScalarGridSpec(
            num_scalar_prefetch=1,
            grid=(outer, wd // count),
            in_specs=[spec, spec],
            out_specs=ospec,
        ),
        out_shape=jax.ShapeDtypeStruct(shape, F32),
        compiler_params=pltpu.CompilerParams(dimension_semantics=("arbitrary", "arbitrary")),
        cost_estimate=cost(0, 3 * wd * outer * size * bw),
        name="finish",
    )(tab, p, q)


def up_pairs(lo, hi):
    return [(2 * p + c, 2 * p + 2 + c) for p in range(lo, hi) for c in range(2)]


def down_pairs(lo, hi):
    return [(2 * p + 2 + c, 2 * p + c) for p in range(lo, hi) for c in range(2)]


def swap(val, n):
    return lax.ppermute(val, "tensor", [(i, i ^ 1) for i in range(n)])


def add(a, b):
    return (a.astype(F32) + b.astype(F32)).astype(BF16)


def line_scatter(parts, nl):
    up, down = parts[nl - 1], parts[1]
    for r in range(1, nl):
        up = lax.ppermute(up, "tensor", up_pairs(0, r))
        down = lax.ppermute(down, "tensor", down_pairs(nl - 1 - r, nl - 1))
        if r < nl - 1:
            up = add(up, parts[nl - 1 - r])
            down = add(down, parts[r + 1])
    return (parts[0].astype(F32) + up.astype(F32) + down.astype(F32)).astype(BF16)


X_PAIRS = [(i, i ^ 1) for i in range(4)]
Y_PAIRS = [(i, i ^ 2) for i in range(4)]


def reduce_dp(keep, send, dp, pairs):
    if dp != 4:
        return lax.psum_scatter(jnp.concatenate([keep, send]), "dp")
    came = lax.ppermute(send, "dp", pairs[0])
    second = lax.ppermute(add(keep[1], came[1]), "dp", pairs[1])
    return (keep[0].astype(F32) + came[0].astype(F32) + second.astype(F32)).astype(BF16)


def gather_dp(val, dp, pairs):
    if dp != 4:
        every = lax.all_gather(val, "dp")
        return every[: dp // 2], every[dp // 2 :]
    low = jnp.stack([val, lax.ppermute(val, "dp", pairs[1])])
    return low, lax.ppermute(low, "dp", pairs[0])


def body(tokens, cotangent, w_first, w_second, w_third, w_fourth):
    rows = tokens.shape[0]
    wd, bw, _ = w_first.shape
    hd = w_second.shape[0]
    n = lax.axis_size("tensor")
    dp = lax.axis_size("dp")
    nl = n // 2
    sub = bw // (wd * n)
    m2 = 2 * hd * sub
    step = m2 // dp
    scale = 1.0 / math.sqrt(rows * dp)
    me = lax.axis_index("tensor")
    mine = lax.axis_index("dp")
    pos, core = me // 2, me % 2
    lines = [[2 * p + c for p in range(nl)] for c in range(2)]
    x_first, y_first = (X_PAIRS, Y_PAIRS), (Y_PAIRS, X_PAIRS)

    dps = jnp.arange(dp, dtype=jnp.int32)
    if dp == 4:
        tab_y = dps ^ mine
        tab_x = ((tab_y & 1) << 1) | (tab_y >> 1)
        inv_x = (((dps & 1) << 1) | (dps >> 1)) ^ mine
        inv_y = tab_y
    else:
        tab_x = tab_y = inv_x = inv_y = dps
    low_end, high_end = pos == 0, pos == nl - 1
    late_pos = jnp.where(low_end, nl - 1, jnp.where(high_end, 0, -1))

    def meta_of(head, late):
        head = jnp.stack([jnp.asarray(v, jnp.int32) for v in (head, core, late_pos, late)])
        return jnp.concatenate([head, inv_x, inv_y])

    w1 = lax.dynamic_index_in_dim(
        w_first.reshape(wd, bw, nl, dp, step), mine, axis=3, keepdims=False
    )
    w4 = lax.dynamic_index_in_dim(
        w_fourth.reshape(wd, nl, dp, step, bw), mine, axis=2, keepdims=False
    )
    w14 = jnp.stack([jnp.transpose(w1, (2, 0, 3, 1)), jnp.transpose(w4, (1, 0, 2, 3))], axis=1)
    w14 = lax.all_to_all(
        w14, "tensor", split_axis=0, concat_axis=0, axis_index_groups=lines, tiled=True
    )
    own, w14 = lax.optimization_barrier((jnp.stack([tokens.T, cotangent.T]), w14))
    ups, downs = [own], [own]
    for r in range(1, nl):
        ups.append(lax.ppermute(ups[-1], "tensor", up_pairs(r - 1, nl - 1)))
        downs.append(lax.ppermute(downs[-1], "tensor", down_pairs(0, nl - r)))
    sides = []
    for e, (pairs, tab) in enumerate(((x_first, tab_x), (y_first, tab_y))):
        every = jnp.concatenate(gather_dp(w14[:, e], dp, pairs))
        every = [lax.dynamic_index_in_dim(every, tab[q], keepdims=False) for q in range(dp)]
        sides.append(jnp.stack(every, axis=2).reshape(nl, wd, m2, bw))
    w14 = jnp.stack(sides)
    slots = [[own], [downs[1]]]
    slots += [[downs[k], ups[nl - k]] for k in range(2, nl - 1)]
    slots += [[ups[1]]]
    late = [ups[nl - 1], downs[nl - 1]]
    metas = [meta_of((pos + k) % nl, 0) for k in range(nl)]
    metas[1] = meta_of((pos + 1) % nl, high_end)
    metas[nl - 1] = meta_of((pos + nl - 1) % nl, low_end)
    late_meta = meta_of(jnp.maximum(late_pos, 0), 0)

    owns, recvs = [], []
    for meta, xg in zip(metas + [late_meta], slots + [late]):
        mine_part, send = expand(meta, xg, w14, hd, sub)
        owns.append(mine_part)
        recvs.append(swap(send, n))
    z_own, z_send, *g23 = middle(
        meta_of(pos, 0), owns, recvs, w_second, w_third, dp, scale
    )
    z_recv = swap(z_send, n)

    parts, grads = [None] * nl, None
    order = [k for pair in zip(range(nl - 1, nl // 2, -1), range(1, nl // 2)) for k in pair]
    for k in order + [nl // 2, 0]:
        xgs = slots[k]
        if k in (1, nl - 1):
            xgs = xgs + [late[0] if k == 1 else late[1]]
        parts[k], *grads = contract(
            metas[k], z_own, z_recv, w14, xgs, k in (1, nl - 1), grads, sub, dp, scale
        )
    both = line_scatter(parts, nl)

    g2 = gather_dp(reduce_dp(*g23[:2], dp, x_first), dp, x_first)
    g3 = gather_dp(reduce_dp(*g23[2:], dp, y_first), dp, y_first)
    g1 = reduce_dp(*grads[:2], dp, x_first)
    g4 = reduce_dp(*grads[2:], dp, y_first)
    g14 = jnp.stack([g1, g4], axis=1)
    g14 = lax.all_to_all(
        g14, "tensor", split_axis=0, concat_axis=0, axis_index_groups=lines, tiled=True
    )
    g1 = gather_dp(g14[:, 0], dp, x_first)
    g4 = gather_dp(g14[:, 1], dp, y_first)

    def single(halves):
        return [h[:, None] for h in halves]

    return (
        both[0].T,
        both[1].T,
        finish(tab_x, g1, True),
        finish(tab_x, single(g2), False),
        finish(tab_y, single(g3), False),
        finish(tab_y, g4, False),
    )


def solution(mesh):
    return jax.shard_map(
        body,
        mesh=mesh,
        in_specs=(
            P("dp", "tensor"),
            P("dp", "tensor"),
            P("tensor", None, None),
            P("tensor", None, None),
            P("tensor", None, None),
            P("tensor", None, None),
        ),
        out_specs=(
            P("dp", "tensor"),
            P("dp", "tensor"),
            P("tensor", None, None),
            P("tensor", None, None),
            P("tensor", None, None),
            P("tensor", None, None),
        ),
        check_vma=False,
    )
```

```python
import functools
import math

import jax
import jax.numpy as jnp
from jax import lax
from jax.experimental import pallas as pl
from jax.experimental.pallas import tpu as pltpu
from jax.sharding import PartitionSpec as P

F32 = jnp.float32
BF16 = jnp.bfloat16
MIDDLE_MIB = 60


def params(mib, dims=1):
    return pltpu.CompilerParams(
        dimension_semantics=("arbitrary",) * dims, vmem_limit_bytes=mib * 1024 * 1024
    )


def gelu_parts(value_in):
    cdf_part = 0.5 * (1.0 + lax.erf(value_in * 0.7071067811865476))
    slope_part = cdf_part + value_in * jnp.exp(-0.5 * value_in * value_in) * 0.3989422804014327
    return (value_in * cdf_part, slope_part)


def dot(a, b, ca, cb):
    return lax.dot_general(a, b, (((ca,), (cb,)), ((), ())), preferred_element_type=F32)


def cost(flops, elements, trans=0):
    return pl.CostEstimate(flops=flops, bytes_accessed=2 * elements, transcendentals=trans)


def assemble_kernel(meta, *refs):
    out_ref = refs[-1]
    _, _, wd, size, bw = out_ref.shape
    step = size // 4
    half = size // 2
    low = meta[0] == 0
    for e in range(4):
        share = lax.bitwise_xor(meta[1], e) * step
        first = refs[e][0, 0] if e < 3 else refs[3][0]
        second = refs[e][0, 1] if e < 3 else refs[4][0]
        left, right = first[:, :, : bw // 2], first[:, :, bw // 2 :]
        first = jnp.concatenate(
            [jnp.where(low, left, right), jnp.where(low, right, left)], axis=2
        )
        out_ref[0, 0, :, pl.ds(pl.multiple_of(share, step), step), :] = first
        row = lax.rem(share + meta[0] * half, size)
        out_ref[1, 0, :, pl.ds(pl.multiple_of(row, step), step), :] = second


def assemble(core, mine, own, by_x, by_y, diag):
    nl, _, wd, step, bw = own.shape
    spec = pl.BlockSpec((1, 2, wd, step, bw), lambda k, meta: (k, 0, 0, 0, 0))
    dspec = pl.BlockSpec((1, wd, step, bw), lambda k, meta: (k, 0, 0, 0))
    return pl.pallas_call(
        assemble_kernel,
        grid_spec=pltpu.PrefetchScalarGridSpec(
            num_scalar_prefetch=1,
            grid=(nl,),
            in_specs=[spec, spec, spec, dspec, dspec],
            out_specs=pl.BlockSpec((2, 1, wd, 4 * step, bw), lambda k, meta: (0, k, 0, 0, 0)),
        ),
        out_shape=jax.ShapeDtypeStruct((2, nl, wd, 4 * step, bw), BF16),
        compiler_params=params(12),
        cost_estimate=cost(0, 16 * nl * wd * step * bw),
        name="assemble",
    )(jnp.stack([core, mine]).astype(jnp.int32), own, by_x, by_y, *diag)


def total(refs, span):
    val = refs[0][span, :]
    for ref in refs[1:]:
        val = val + ref[span, :]
    return val


def weight_spec(side, w14s, pa):
    same = w14s[0] is w14s[1]
    shape = (1, 1, pa, *w14s[side].shape[3:])
    return pl.BlockSpec(shape, lambda s, meta: (side if same else 0, meta[0], s, 0, 0))


def expand_kernel(meta, *refs, side, pa, bw, hd, sub):
    x_refs, (w_ref, own_ref, send_ref) = refs[:-3], refs[-3:]
    m = hd * sub
    own, send = [], []
    for a in range(pa):
        x = total(x_refs, slice(a * bw, (a + 1) * bw))
        val = dot(w_ref[0, 0, a], x, side, 0)
        own.append(val[:m].reshape(hd, sub, val.shape[-1]))
        send.append(val[m:].reshape(hd, sub, val.shape[-1]))
    own_ref[...] = jnp.concatenate(own, axis=1).astype(BF16)
    send_ref[...] = jnp.concatenate(send, axis=1).astype(BF16)


def expand(side, meta, xs, w14s, hd, sub):
    _, nl, wd, m2, bw = w14s[1].shape
    rows = xs[0].shape[-1]
    pa = min(wd, 2)
    out = jax.ShapeDtypeStruct((hd, wd * sub, rows), BF16)
    out_spec = pl.BlockSpec((hd, pa * sub, rows), lambda s, meta: (0, s, 0))
    return pl.pallas_call(
        functools.partial(expand_kernel, side=side, pa=pa, bw=bw, hd=hd, sub=sub),
        grid_spec=pltpu.PrefetchScalarGridSpec(
            num_scalar_prefetch=1,
            grid=(wd // pa,),
            in_specs=[pl.BlockSpec((pa * bw, rows), lambda s, meta: (s, 0))] * len(xs)
            + [weight_spec(side, w14s, pa)],
            out_specs=[out_spec, out_spec],
        ),
        out_shape=[out, out],
        compiler_params=params(12),
        cost_estimate=cost(2 * wd * m2 * bw * rows, wd * (bw * rows + m2 * bw + m2 * rows)),
        name="expand",
    )(meta, *xs, w14s[side])


def put_shares(meta, first, gsc, val, keep_ref, send_ref, index, dp):
    step = val.shape[0] // dp
    gsc[...] = val.astype(gsc.dtype)
    half = dp // 2
    for p in range(dp):
        row = pl.multiple_of(meta[first + p] * step, step)
        ref = keep_ref if p < half else send_ref
        ref[(p % half, *index)] = gsc[pl.ds(row, step), :].astype(BF16)


def join(pieces):
    if pieces[0].shape[0] % 16:
        return jnp.concatenate([p.astype(F32) for p in pieces], axis=0).astype(BF16)
    return jnp.concatenate(pieces, axis=0)


def rows_of(meta, sides, b, nl):
    pieces = []
    for k in range(nl):
        for side in sides:
            val = side[k][b]
            if k in (1, nl - 1):
                val = jnp.where(meta[2] == k, side[nl][b], val)
            pieces.append(val)
    return join(pieces)


def split_cores(val, own_ref, send_ref, b, nl, part):
    for k in range(nl):
        own_ref[b, k * part : (k + 1) * part] = val[2 * k * part : (2 * k + 1) * part].astype(BF16)
        send_ref[b, k * part : (k + 1) * part] = val[(2 * k + 1) * part : (2 * k + 2) * part].astype(BF16)


def forward_kernel(meta, *refs, nl, part, hb):
    sides = (refs[: nl + 1], refs[nl + 1 : 2 * nl + 2])
    w2_ref, w3_ref, own_ref, send_ref, y_ref, act_ref, slope_ref = refs[2 * nl + 2 :]
    for b in range(hb):
        yb = rows_of(meta, sides, b, nl)
        y_ref[b] = yb
        val, slope = gelu_parts(dot(w2_ref[b], yb, 0, 0))
        act = val.astype(BF16)
        act_ref[b] = act
        slope_ref[b] = slope.astype(BF16)
        split_cores(dot(w3_ref[b], act, 1, 0), own_ref, send_ref, b, nl, part)


def backward_kernel(meta, *refs, nl, part, hb, dp, scale):
    sides = (refs[: nl + 1], refs[nl + 1 : 2 * nl + 2])
    refs = refs[2 * nl + 2 :]
    w2_ref, w3_ref, y_ref, act_ref, slope_ref, own_ref, send_ref = refs[:7]
    g2k_ref, g2s_ref, g3k_ref, g3s_ref, gsc = refs[7:]
    for b in range(hb):
        dzb = rows_of(meta, sides, b, nl)
        dact = dot(w3_ref[b], dzb, 0, 0)
        dpre = (dact * slope_ref[b].astype(F32)).astype(BF16)
        split_cores(dot(w2_ref[b], dpre, 1, 0), own_ref, send_ref, b, nl, part)
        put_shares(meta, 4, gsc.at[b, 0], dot(y_ref[b], dpre, 1, 1) * scale, g2k_ref, g2s_ref, (b,), dp)
        put_shares(
            meta, 4 + dp, gsc.at[b, 1], dot(dzb, act_ref[b], 1, 1) * scale, g3k_ref, g3s_ref, (b,), dp
        )


def middle(back, meta, owns, recvs, w2, w3, saved, dp, scale):
    hd, k, j = w2.shape
    nl = len(owns) - 1
    _, part, rows = owns[0].shape
    hb = 2
    half = dp // 2
    slot = pl.BlockSpec((hb, part, rows), lambda b, meta: (b, 0, 0))
    one = pl.BlockSpec((hb, nl * part, rows), lambda b, meta: (b, 0, 0))
    full = pl.BlockSpec((hb, k, rows), lambda b, meta: (b, 0, 0))
    wspec = pl.BlockSpec((hb, k, j), lambda b, meta: (b, 0, 0))
    gspec = pl.BlockSpec((half, hb, k // dp, j), lambda b, meta: (0, b, 0, 0))
    zout = jax.ShapeDtypeStruct((hd, nl * part, rows), BF16)
    yout = jax.ShapeDtypeStruct((hd, k, rows), BF16)
    gout = jax.ShapeDtypeStruct((half, hd, k // dp, j), BF16)
    gtype = BF16 if (k // dp) % 16 == 0 else F32
    in_specs = [slot] * (2 * nl + 2) + [wspec, wspec]
    if back:
        body = functools.partial(backward_kernel, nl=nl, part=part, hb=hb, dp=dp, scale=scale)
        in_specs += [full] * 3
        out_specs, out_shape = [one] * 2 + [gspec] * 4, [zout] * 2 + [gout] * 4
        scratch = [pltpu.VMEM((hb, 2, k, j), gtype)]
        work = cost(8 * hd * k * j * rows, 5 * hd * k * rows + 4 * hd * k * j)
    else:
        body = functools.partial(forward_kernel, nl=nl, part=part, hb=hb)
        out_specs, out_shape = [one] * 2 + [full] * 3, [zout] * 2 + [yout] * 3
        scratch = []
        work = cost(4 * hd * k * j * rows, 5 * hd * k * rows + 2 * hd * k * j, 2 * hd * j * rows)
    return pl.pallas_call(
        body,
        grid_spec=pltpu.PrefetchScalarGridSpec(
            num_scalar_prefetch=1,
            grid=(hd // hb,),
            in_specs=in_specs,
            out_specs=out_specs,
            scratch_shapes=scratch,
        ),
        out_shape=out_shape,
        compiler_params=params(MIDDLE_MIB),
        cost_estimate=work,
        name="backward" if back else "forward",
    )(meta, *owns, *recvs, w2, w3, *saved)


def block_rows(own_ref, recv_ref, pa, hd, sub):
    wide = [ref[...].astype(F32) for ref in (own_ref, recv_ref)]
    rows = wide[0].shape[-1]
    return [
        jnp.concatenate(
            [v[:, a * sub : (a + 1) * sub, :].reshape(hd * sub, rows) for v in wide], axis=0
        ).astype(BF16)
        for a in range(pa)
    ]


def output_kernel(meta, zo_ref, zr_ref, w4_ref, out_ref, *, pa, bw, hd, sub):
    for a, z in enumerate(block_rows(zo_ref, zr_ref, pa, hd, sub)):
        out_ref[0, a * bw : (a + 1) * bw, :] = dot(w4_ref[0, 0, a], z, 0, 0).astype(BF16)


def output_parts(meta, z_own, z_recv, w14s, sub):
    same = w14s[0] is w14s[1]
    w4 = w14s[1]
    _, nl, wd, m2, bw = w4.shape
    hd, _, rows = z_own.shape
    pa = min(wd, 2)
    steps = wd // pa
    zspec = pl.BlockSpec((hd, pa * sub, rows), lambda k, s, meta: (0, k * steps + s, 0))
    wspec = pl.BlockSpec(
        (1, 1, pa, m2, bw), lambda k, s, meta: (1 if same else 0, meta[k], s, 0, 0)
    )
    return pl.pallas_call(
        functools.partial(output_kernel, pa=pa, bw=bw, hd=hd, sub=sub),
        grid_spec=pltpu.PrefetchScalarGridSpec(
            num_scalar_prefetch=1,
            grid=(nl, steps),
            in_specs=[zspec, zspec, wspec],
            out_specs=pl.BlockSpec((1, pa * bw, rows), lambda k, s, meta: (meta[k], s, 0)),
        ),
        out_shape=jax.ShapeDtypeStruct((nl, wd * bw, rows), BF16),
        compiler_params=params(16, 2),
        cost_estimate=cost(2 * nl * wd * m2 * bw * rows, nl * wd * (bw * rows + m2 * rows + m2 * bw)),
        name="output",
    )(meta, z_own, z_recv, w4)


def contract_kernel(meta, *refs, nx, late, chain, pa, bw, hd, sub, dp, scale):
    zo_ref, zr_ref, dyo_ref, dyr_ref, w1_ref = refs[:5]
    x_refs, g_refs = refs[5 : 5 + nx], refs[5 + nx : 5 + 2 * nx]
    refs = refs[5 + 2 * nx + (4 if chain else 0) :]
    part_ref, g1k_ref, g1s_ref, g4k_ref, g4s_ref, gsc = refs
    zs = block_rows(zo_ref, zr_ref, pa, hd, sub)
    dys = block_rows(dyo_ref, dyr_ref, pa, hd, sub)

    def shard(refs, span):
        if late:
            return jnp.where(meta[3] > 0, refs[1][span, :], refs[0][span, :])
        return total(refs, span)

    for a in range(pa):
        span = slice(a * bw, (a + 1) * bw)
        z, dy = zs[a], dys[a]
        part_ref[span, :] = dot(w1_ref[0, 0, a], dy, 1, 0).astype(BF16)
        g1 = dot(dy, shard(x_refs, span), 1, 1) * scale
        g4 = dot(z, shard(g_refs, span), 1, 1) * scale
        put_shares(meta, 4, gsc.at[a, 0], g1, g1k_ref, g1s_ref, (0, a), dp)
        put_shares(meta, 4 + dp, gsc.at[a, 1], g4, g4k_ref, g4s_ref, (0, a), dp)


def contract(k, meta, zdy, w14s, xs, gs, late, grads, sub, dp, scale):
    _, nl, wd, m2, bw = w14s[1].shape
    hd, _, rows = zdy[0].shape
    pa = min(wd, 2)
    steps = wd // pa
    half = dp // 2
    zspec = pl.BlockSpec((hd, pa * sub, rows), lambda s, meta: (0, k * steps + s, 0))
    xspec = pl.BlockSpec((pa * bw, rows), lambda s, meta: (s, 0))
    gspec = pl.BlockSpec((half, 1, pa, m2 // dp, bw), lambda s, meta: (0, meta[0], s, 0, 0))
    gout = jax.ShapeDtypeStruct((half, nl, wd, m2 // dp, bw), BF16)
    gtype = BF16 if (m2 // dp) % 16 == 0 else F32
    args = [meta, *zdy, w14s[0], *xs, *gs]
    specs = [zspec] * 4 + [weight_spec(0, w14s, pa)] + [xspec] * (2 * len(xs))
    aliases = {}
    if grads is not None:
        aliases = {len(args) + i: 1 + i for i in range(4)}
        args += list(grads)
        specs += [pl.BlockSpec(memory_space=pl.ANY)] * 4
    return pl.pallas_call(
        functools.partial(
            contract_kernel,
            nx=len(xs),
            late=late,
            chain=grads is not None,
            pa=pa,
            bw=bw,
            hd=hd,
            sub=sub,
            dp=dp,
            scale=scale,
        ),
        grid_spec=pltpu.PrefetchScalarGridSpec(
            num_scalar_prefetch=1,
            grid=(steps,),
            in_specs=specs,
            out_specs=[xspec, gspec, gspec, gspec, gspec],
            scratch_shapes=[pltpu.VMEM((pa, 2, m2, bw), gtype)],
        ),
        out_shape=[jax.ShapeDtypeStruct(xs[0].shape, BF16), gout, gout, gout, gout],
        input_output_aliases=aliases,
        compiler_params=params(20),
        cost_estimate=cost(
            6 * wd * m2 * bw * rows, wd * (3 * bw * rows + 2 * m2 * rows + 3 * m2 * bw)
        ),
        name="contract",
    )(*args)


def finish_kernel(tab, *refs, dp, piece, flip):
    val_refs, o_ref, sc = refs[:dp], refs[dp], refs[dp + 1]
    count = o_ref.shape[0]
    for a in range(count):
        for e in range(dp):
            val = val_refs[e][0, a].astype(F32)
            step = val.shape[0]
            share = lax.bitwise_xor(tab[0], e) * (step // piece)
            for i in range(step // piece):
                row = pl.multiple_of(tab[1 + share + i], piece)
                if flip:
                    sc[pl.ds(row, piece), :] = val[i * piece : (i + 1) * piece]
                else:
                    o_ref[a, pl.ds(row, piece), :] = val[i * piece : (i + 1) * piece]
        if flip:
            o_ref[a] = sc[...].T


def finish(tab, shares, flip):
    dp = len(shares)
    outer, wd, step, bw = shares[0].shape
    size = dp * step
    pieces = tab.shape[0] - 1
    piece = size // pieces
    count = min(wd, 4)
    if flip and size % 128:
        base = tab[0]
        merged = jnp.stack(shares)[jnp.arange(dp) ^ base]
        merged = jnp.transpose(merged, (1, 2, 0, 3, 4)).reshape(outer, wd, pieces, piece, bw)
        merged = merged[:, :, jnp.argsort(tab[1:])].reshape(outer, wd, size, bw)
        return jnp.transpose(merged, (1, 3, 0, 2)).reshape(wd, bw, outer * size).astype(F32)
    spec = pl.BlockSpec((1, count, step, bw), lambda o, a, tab: (o, a, 0, 0))
    if flip:
        shape = (wd, bw, outer * size)
        ospec = pl.BlockSpec((count, bw, size), lambda o, a, tab: (a, 0, o))
    else:
        shape = (wd, outer * size, bw)
        ospec = pl.BlockSpec((count, size, bw), lambda o, a, tab: (a, o, 0))
    return pl.pallas_call(
        functools.partial(finish_kernel, dp=dp, piece=piece, flip=flip),
        grid_spec=pltpu.PrefetchScalarGridSpec(
            num_scalar_prefetch=1,
            grid=(outer, wd // count),
            in_specs=[spec] * dp,
            out_specs=ospec,
            scratch_shapes=[pltpu.VMEM((size, bw), F32)],
        ),
        out_shape=jax.ShapeDtypeStruct(shape, F32),
        compiler_params=params(12, 2),
        cost_estimate=cost(0, 3 * wd * outer * size * bw),
        name="finish",
    )(tab, *shares)


def close_kernel(a_ref, b_ref, c_ref, out_ref):
    val = a_ref[...].astype(F32) + b_ref[...].astype(F32) + c_ref[...].astype(F32)
    out_ref[...] = val.T.astype(BF16)


def close(a, b, c):
    width, rows = a.shape
    block = min(width, 256)
    return pl.pallas_call(
        close_kernel,
        grid=(width // block,),
        in_specs=[pl.BlockSpec((block, rows), lambda s: (s, 0))] * 3,
        out_specs=pl.BlockSpec((rows, block), lambda s: (0, s)),
        out_shape=jax.ShapeDtypeStruct((rows, width), BF16),
        compiler_params=params(12),
        cost_estimate=cost(2 * width * rows, 4 * width * rows),
        name="close",
    )(a, b, c)


def up_pairs(lo, hi):
    return [(2 * p + c, 2 * p + 2 + c) for p in range(lo, hi) for c in range(2)]


def down_pairs(lo, hi):
    return [(2 * p + 2 + c, 2 * p + c) for p in range(lo, hi) for c in range(2)]


def swap(val, n):
    return lax.ppermute(val, "tensor", [(i, i ^ 1) for i in range(n)])


def add(a, b):
    return (a.astype(F32) + b.astype(F32)).astype(BF16)


X_PAIRS = [(i, i ^ 1) for i in range(4)]
Y_PAIRS = [(i, i ^ 2) for i in range(4)]


def reduce_dp(grads, dp, orders):
    if dp != 4:
        return [lax.psum_scatter(jnp.concatenate(pair), "dp") for pair in grads]
    came = [lax.ppermute(g[1], "dp", p[0]) for g, p in zip(grads, orders)]
    second = [add(g[0][1], c[1]) for g, c in zip(grads, came)]
    second = lax.optimization_barrier(second)
    second = [lax.ppermute(v, "dp", p[1]) for v, p in zip(second, orders)]
    return [
        (g[0][0].astype(F32) + c[0].astype(F32) + v.astype(F32)).astype(BF16)
        for g, c, v in zip(grads, came, second)
    ]


def gather_dp(val, dp, x_last):
    if dp != 4:
        every = lax.all_gather(val, "dp")
        return [every[q] for q in range(dp)]
    by_x = lax.ppermute(val, "dp", X_PAIRS)
    by_y = lax.ppermute(val, "dp", Y_PAIRS)
    if x_last:
        diag = lax.ppermute(by_y, "dp", X_PAIRS)
    else:
        diag = lax.ppermute(by_x, "dp", Y_PAIRS)
    return [val, by_x, by_y, diag]


def body(tokens, cotangent, w_first, w_second, w_third, w_fourth):
    rows = tokens.shape[0]
    wd, bw, _ = w_first.shape
    hd = w_second.shape[0]
    n = lax.axis_size("tensor")
    dp = lax.axis_size("dp")
    nl = n // 2
    sub = bw // (wd * n)
    part = wd * sub
    m = hd * sub
    m2 = 2 * m
    step = m2 // dp
    scale = 1.0 / math.sqrt(rows * dp)
    me = lax.axis_index("tensor")
    mine = lax.axis_index("dp")
    pos, core = me // 2, me % 2
    lines = [[2 * p + c for p in range(nl)] for c in range(2)]
    x_first, y_first = (X_PAIRS, Y_PAIRS), (Y_PAIRS, X_PAIRS)

    dps = jnp.arange(dp, dtype=jnp.int32)
    if dp == 4:
        inv_x = (((dps & 1) << 1) | (dps >> 1)) ^ mine
        inv_y = dps ^ mine
        base = mine
    else:
        inv_x = inv_y = dps
        base = mine * 0
    low_end, high_end = pos == 0, pos == nl - 1
    late_slot = jnp.where(low_end, nl - 1, jnp.where(high_end, 1, -1))

    def meta_of(head, late):
        head = jnp.stack([jnp.asarray(v, jnp.int32) for v in (head, core, late_slot, late)])
        return jnp.concatenate([head, inv_x, inv_y])

    w1 = lax.dynamic_index_in_dim(
        w_first.reshape(wd, dp, bw // dp, nl * m2), mine, axis=1, keepdims=False
    )
    w4 = lax.dynamic_index_in_dim(
        w_fourth.reshape(wd, nl, dp, step, bw), mine, axis=2, keepdims=False
    )
    if m2 == bw:
        w1 = w1.reshape(wd, step, nl, bw)
        w14 = jnp.stack([jnp.transpose(w1, (2, 0, 1, 3)), jnp.transpose(w4, (1, 0, 2, 3))], axis=1)
        w14 = lax.all_to_all(
            w14, "tensor", split_axis=0, concat_axis=0, axis_index_groups=lines, tiled=True
        )
        sides = [w14[:, 0], w14[:, 1]]
    else:
        w1 = jnp.transpose(w1.reshape(wd, bw // dp, nl, m2), (2, 0, 1, 3))
        w4 = jnp.transpose(w4, (1, 0, 2, 3))
        sides = [
            lax.all_to_all(
                w, "tensor", split_axis=0, concat_axis=0, axis_index_groups=lines, tiled=True
            )
            for w in (w1, w4)
        ]
    x_own, g_own = tokens.T, cotangent.T
    x_own, sides = lax.optimization_barrier((x_own, sides))
    whole = dp == 4 and m2 == bw
    if whole:
        by_x = lax.ppermute(w14, "dp", X_PAIRS)
        by_y = lax.ppermute(w14, "dp", Y_PAIRS)
        gate = [by_x, by_y]
    else:
        gate = [lax.all_gather(w, "dp") for w in sides]

    def relative(w):
        w = w.reshape(hd, nl, 2, part, bw)
        w = jnp.where(core == 0, w, w[:, :, ::-1])
        w = lax.dynamic_slice_in_dim(jnp.concatenate([w, w], axis=1), pos, nl, axis=1)
        return w.reshape(hd, bw, bw)

    w2 = relative(w_second)
    w3 = relative(jnp.swapaxes(w_third, 1, 2))

    def hop(ups, downs, r):
        up = lax.ppermute(ups[-1], "tensor", up_pairs(r - 1, nl - 1))
        down = lax.ppermute(downs[-1], "tensor", down_pairs(0, nl - r))
        return up, down

    x_ups, x_downs = [x_own], [x_own]
    for r in range(1, nl):
        up, down = hop(x_ups, x_downs, r)
        if r == 1:
            up, down, gate, w2, w3 = lax.optimization_barrier((up, down, gate, w2, w3))
            if whole:
                by_x, by_y = gate
                gate = [
                    lax.ppermute(by_y[:, 0], "dp", X_PAIRS),
                    lax.ppermute(by_x[:, 1], "dp", Y_PAIRS),
                ]
        elif r == 2:
            up, down, gate, g_own = lax.optimization_barrier((up, down, gate, g_own))
        x_ups.append(up)
        x_downs.append(down)
    g_ups, g_downs = [g_own], [g_own]
    for r in range(1, nl):
        up, down = hop(g_ups, g_downs, r)
        up, down = lax.optimization_barrier((up, down))
        g_ups.append(up)
        g_downs.append(down)
    if whole:
        w14s = (assemble(core, mine, w14, by_x, by_y, gate),) * 2
    else:
        w1, w4 = gate
        w1 = jnp.transpose(w1, (1, 2, 0, 3, 4)).reshape(nl, wd, bw, 2, m)
        w4 = jnp.transpose(w4, (1, 2, 0, 3, 4)).reshape(nl, wd, 2, m, bw)
        w1 = jnp.where(core == 0, w1, w1[:, :, :, ::-1]).reshape(nl, wd, bw, m2)
        w4 = jnp.where(core == 0, w4, w4[:, :, ::-1]).reshape(nl, wd, m2, bw)
        w14s = (w1[None], w4[None])

    def slots_of(ups, downs):
        slots = [[ups[0]], [downs[1]]]
        slots += [[downs[k], ups[nl - k]] for k in range(2, nl - 1)]
        return slots + [[ups[1]], [ups[nl - 1], downs[nl - 1]]]

    metas = [meta_of((pos + k) % nl, 0) for k in range(nl)]
    metas[1] = meta_of((pos + 1) % nl, high_end)
    metas[nl - 1] = meta_of((pos + nl - 1) % nl, low_end)
    metas.append(meta_of(jnp.where(low_end, nl - 1, 0), 0))

    def first_factor(side, slots):
        owns, recvs = [], []
        for meta, xs in zip(metas, slots):
            mine_part, send = expand(side, meta, xs, w14s, hd, sub)
            owns.append(mine_part)
            recvs.append(swap(send, n))
        return owns, recvs

    x_slots, g_slots = slots_of(x_ups, x_downs), slots_of(g_ups, g_downs)
    owns, recvs = first_factor(0, x_slots)
    z_own, z_send, *saved = middle(False, metas[0], owns, recvs, w2, w3, [], dp, scale)
    z_recv = swap(z_send, n)
    places = ((pos + jnp.arange(nl)) % nl).astype(jnp.int32)
    outs = output_parts(places, z_own, z_recv, w14s, sub)
    layer_out = lax.psum_scatter(outs, "tensor", axis_index_groups=lines).T

    owns, recvs = first_factor(1, g_slots)
    dy_own, dy_send, *g23 = middle(True, metas[0], owns, recvs, w2, w3, saved, dp, scale)
    dy_recv = swap(dy_send, n)
    parts, grads = [None] * nl, None
    order = [k for pair in zip(range(nl - 1, nl // 2, -1), range(1, nl // 2)) for k in pair]
    for k in order + [nl // 2, 0]:
        late = k in (1, nl - 1)
        xs, gs = x_slots[k], g_slots[k]
        if late:
            xs = xs + [x_slots[nl][0 if k == 1 else 1]]
            gs = gs + [g_slots[nl][0 if k == 1 else 1]]
        parts[k], *grads = contract(
            k,
            metas[k],
            (z_own, z_recv, dy_own, dy_recv),
            w14s,
            xs,
            gs,
            late,
            grads,
            sub,
            dp,
            scale,
        )

    g1, g2, g3, g4 = reduce_dp(
        [grads[:2], g23[:2], g23[2:], grads[2:]], dp, (x_first, x_first, y_first, y_first)
    )
    g14 = jnp.stack([g1, g4], axis=1)
    g14 = lax.all_to_all(
        g14, "tensor", split_axis=0, concat_axis=0, axis_index_groups=lines, tiled=True
    )

    up, down = parts[nl - 1], parts[1]
    for r in range(1, nl):
        if r == nl - 1:
            up, down, g14 = lax.optimization_barrier((up, down, g14))
        up = lax.ppermute(up, "tensor", up_pairs(0, r))
        down = lax.ppermute(down, "tensor", down_pairs(nl - 1 - r, nl - 1))
        if r < nl - 1:
            up = add(up, parts[nl - 1 - r])
            down = add(down, parts[r + 1])
            up, down = lax.optimization_barrier((up, down))

    g2 = gather_dp(g2, dp, True)
    g3 = gather_dp(g3, dp, False)
    g1 = gather_dp(g14[:, 0], dp, True)
    g4 = gather_dp(g14[:, 1], dp, False)
    tokens_grad = close(parts[0], up, down)

    base = jnp.asarray(base, jnp.int32)[None]
    offset = jnp.arange(2 * nl, dtype=jnp.int32)
    wide_rows = (((offset // 2 + pos) % nl) * 2 + (offset + core) % 2) * part
    dual_rows = (jnp.arange(dp, dtype=jnp.int32) * step + core * m) % m2
    wide_tab = jnp.concatenate([base, wide_rows.astype(jnp.int32)])
    dual_tab = jnp.concatenate([base, dual_rows.astype(jnp.int32)])
    out_two = finish(wide_tab, [g[None] for g in g2], False)
    out_three = finish(wide_tab, [g[None] for g in g3], True)
    g1, g4, out_two, out_three = lax.optimization_barrier((g1, g4, out_two, out_three))
    return (
        layer_out,
        tokens_grad,
        finish(dual_tab, g1, True),
        out_two,
        out_three,
        finish(dual_tab, g4, False),
    )


def solution(mesh):
    return jax.shard_map(
        body,
        mesh=mesh,
        in_specs=(
            P("dp", "tensor"),
            P("dp", "tensor"),
            P("tensor", None, None),
            P("tensor", None, None),
            P("tensor", None, None),
            P("tensor", None, None),
        ),
        out_specs=(
            P("dp", "tensor"),
            P("dp", "tensor"),
            P("tensor", None, None),
            P("tensor", None, None),
            P("tensor", None, None),
            P("tensor", None, None),
        ),
        check_vma=False,
    )
```

```python
import functools
import math

import jax
import jax.numpy as jnp
from jax import lax
from jax.experimental import pallas as pl
from jax.experimental.pallas import tpu as pltpu
from jax.sharding import PartitionSpec as P

F32 = jnp.float32
BF16 = jnp.bfloat16
MIDDLE_MIB = 60


def params(mib, dims=1):
    return pltpu.CompilerParams(
        dimension_semantics=("arbitrary",) * dims, vmem_limit_bytes=mib * 1024 * 1024
    )


def gelu_parts(value_in):
    cdf_part = 0.5 * (1.0 + lax.erf(value_in * 0.7071067811865476))
    slope_part = cdf_part + value_in * jnp.exp(-0.5 * value_in * value_in) * 0.3989422804014327
    return (value_in * cdf_part, slope_part)


def dot(a, b, ca, cb):
    return lax.dot_general(a, b, (((ca,), (cb,)), ((), ())), preferred_element_type=F32)


def cost(flops, elements, trans=0):
    return pl.CostEstimate(flops=flops, bytes_accessed=2 * elements, transcendentals=trans)


def assemble_kernel(meta, *refs):
    out_ref = refs[-1]
    _, _, wd, size, bw = out_ref.shape
    step = size // 4
    half = size // 2
    low = meta[0] == 0
    for e in range(4):
        share = lax.bitwise_xor(meta[1], e) * step
        first = refs[e][0, 0] if e < 3 else refs[3][0]
        second = refs[e][0, 1] if e < 3 else refs[4][0]
        left, right = first[:, :, : bw // 2], first[:, :, bw // 2 :]
        first = jnp.concatenate(
            [jnp.where(low, left, right), jnp.where(low, right, left)], axis=2
        )
        out_ref[0, 0, :, pl.ds(pl.multiple_of(share, step), step), :] = first
        row = lax.rem(share + meta[0] * half, size)
        out_ref[1, 0, :, pl.ds(pl.multiple_of(row, step), step), :] = second


def assemble(core, mine, own, by_x, by_y, diag):
    nl, _, wd, step, bw = own.shape
    spec = pl.BlockSpec((1, 2, wd, step, bw), lambda k, meta: (k, 0, 0, 0, 0))
    dspec = pl.BlockSpec((1, wd, step, bw), lambda k, meta: (k, 0, 0, 0))
    return pl.pallas_call(
        assemble_kernel,
        grid_spec=pltpu.PrefetchScalarGridSpec(
            num_scalar_prefetch=1,
            grid=(nl,),
            in_specs=[spec, spec, spec, dspec, dspec],
            out_specs=pl.BlockSpec((2, 1, wd, 4 * step, bw), lambda k, meta: (0, k, 0, 0, 0)),
        ),
        out_shape=jax.ShapeDtypeStruct((2, nl, wd, 4 * step, bw), BF16),
        compiler_params=params(12),
        cost_estimate=cost(0, 16 * nl * wd * step * bw),
        name="assemble",
    )(jnp.stack([core, mine]).astype(jnp.int32), own, by_x, by_y, *diag)


def total(refs, span):
    val = refs[0][span, :]
    for ref in refs[1:]:
        val = val + ref[span, :]
    return val


def weight_spec(side, w14s, pa):
    same = w14s[0] is w14s[1]
    shape = (1, 1, pa, *w14s[side].shape[3:])
    return pl.BlockSpec(shape, lambda s, meta: (side if same else 0, meta[0], s, 0, 0))


def expand_kernel(meta, *refs, side, pa, bw, hd, sub):
    x_refs, (w_ref, own_ref, send_ref) = refs[:-3], refs[-3:]
    m = hd * sub
    own, send = [], []
    for a in range(pa):
        x = total(x_refs, slice(a * bw, (a + 1) * bw))
        val = dot(w_ref[0, 0, a], x, side, 0)
        own.append(val[:m].reshape(hd, sub, val.shape[-1]))
        send.append(val[m:].reshape(hd, sub, val.shape[-1]))
    own_ref[...] = jnp.concatenate(own, axis=1).astype(BF16)
    send_ref[...] = jnp.concatenate(send, axis=1).astype(BF16)


def expand(side, meta, xs, w14s, hd, sub):
    _, nl, wd, m2, bw = w14s[1].shape
    rows = xs[0].shape[-1]
    pa = min(wd, 2)
    out = jax.ShapeDtypeStruct((hd, wd * sub, rows), BF16)
    out_spec = pl.BlockSpec((hd, pa * sub, rows), lambda s, meta: (0, s, 0))
    return pl.pallas_call(
        functools.partial(expand_kernel, side=side, pa=pa, bw=bw, hd=hd, sub=sub),
        grid_spec=pltpu.PrefetchScalarGridSpec(
            num_scalar_prefetch=1,
            grid=(wd // pa,),
            in_specs=[pl.BlockSpec((pa * bw, rows), lambda s, meta: (s, 0))] * len(xs)
            + [weight_spec(side, w14s, pa)],
            out_specs=[out_spec, out_spec],
        ),
        out_shape=[out, out],
        compiler_params=params(12),
        cost_estimate=cost(2 * wd * m2 * bw * rows, wd * (bw * rows + m2 * bw + m2 * rows)),
        name="expand",
    )(meta, *xs, w14s[side])


def put_shares(meta, first, gsc, val, keep_ref, send_ref, index, dp):
    step = val.shape[0] // dp
    gsc[...] = val.astype(gsc.dtype)
    half = dp // 2
    for p in range(dp):
        row = pl.multiple_of(meta[first + p] * step, step)
        ref = keep_ref if p < half else send_ref
        ref[(p % half, *index)] = gsc[pl.ds(row, step), :].astype(BF16)


def join(pieces):
    if pieces[0].shape[0] % 16:
        return jnp.concatenate([p.astype(F32) for p in pieces], axis=0).astype(BF16)
    return jnp.concatenate(pieces, axis=0)


def rows_of(meta, sides, b, nl):
    pieces = []
    for k in range(nl):
        for side in sides:
            val = side[k][b]
            if k in (1, nl - 1):
                val = jnp.where(meta[2] == k, side[nl][b], val)
            pieces.append(val)
    return join(pieces)


def split_cores(val, own_ref, send_ref, b, nl, part):
    for k in range(nl):
        own_ref[b, k * part : (k + 1) * part] = val[2 * k * part : (2 * k + 1) * part].astype(BF16)
        send_ref[b, k * part : (k + 1) * part] = val[(2 * k + 1) * part : (2 * k + 2) * part].astype(BF16)


def forward_kernel(meta, *refs, nl, part, hb):
    sides = (refs[: nl + 1], refs[nl + 1 : 2 * nl + 2])
    w2_ref, w3_ref, own_ref, send_ref, y_ref, act_ref, slope_ref = refs[2 * nl + 2 :]
    for b in range(hb):
        yb = rows_of(meta, sides, b, nl)
        y_ref[b] = yb
        val, slope = gelu_parts(dot(w2_ref[b], yb, 0, 0))
        act = val.astype(BF16)
        act_ref[b] = act
        slope_ref[b] = slope.astype(BF16)
        split_cores(dot(w3_ref[b], act, 1, 0), own_ref, send_ref, b, nl, part)


def backward_kernel(meta, *refs, nl, part, hb, dp, scale):
    sides = (refs[: nl + 1], refs[nl + 1 : 2 * nl + 2])
    refs = refs[2 * nl + 2 :]
    w2_ref, w3_ref, y_ref, act_ref, slope_ref, own_ref, send_ref = refs[:7]
    g2k_ref, g2s_ref, g3k_ref, g3s_ref, gsc = refs[7:]
    for b in range(hb):
        dzb = rows_of(meta, sides, b, nl)
        dact = dot(w3_ref[b], dzb, 0, 0)
        dpre = (dact * slope_ref[b].astype(F32)).astype(BF16)
        split_cores(dot(w2_ref[b], dpre, 1, 0), own_ref, send_ref, b, nl, part)
        put_shares(meta, 4, gsc.at[b, 0], dot(y_ref[b], dpre, 1, 1) * scale, g2k_ref, g2s_ref, (b,), dp)
        put_shares(
            meta, 4 + dp, gsc.at[b, 1], dot(dzb, act_ref[b], 1, 1) * scale, g3k_ref, g3s_ref, (b,), dp
        )


def middle(back, meta, owns, recvs, w2, w3, saved, dp, scale):
    hd, k, j = w2.shape
    nl = len(owns) - 1
    _, part, rows = owns[0].shape
    hb = 4
    half = dp // 2
    slot = pl.BlockSpec((hb, part, rows), lambda b, meta: (b, 0, 0))
    one = pl.BlockSpec((hb, nl * part, rows), lambda b, meta: (b, 0, 0))
    full = pl.BlockSpec((hb, k, rows), lambda b, meta: (b, 0, 0))
    wspec = pl.BlockSpec((hb, k, j), lambda b, meta: (b, 0, 0))
    gspec = pl.BlockSpec((half, hb, k // dp, j), lambda b, meta: (0, b, 0, 0))
    zout = jax.ShapeDtypeStruct((hd, nl * part, rows), BF16)
    yout = jax.ShapeDtypeStruct((hd, k, rows), BF16)
    gout = jax.ShapeDtypeStruct((half, hd, k // dp, j), BF16)
    gtype = BF16 if (k // dp) % 16 == 0 else F32
    in_specs = [slot] * (2 * nl + 2) + [wspec, wspec]
    if back:
        body = functools.partial(backward_kernel, nl=nl, part=part, hb=hb, dp=dp, scale=scale)
        in_specs += [full] * 3
        out_specs, out_shape = [one] * 2 + [gspec] * 4, [zout] * 2 + [gout] * 4
        scratch = [pltpu.VMEM((hb, 2, k, j), gtype)]
        work = cost(8 * hd * k * j * rows, 5 * hd * k * rows + 4 * hd * k * j)
    else:
        body = functools.partial(forward_kernel, nl=nl, part=part, hb=hb)
        out_specs, out_shape = [one] * 2 + [full] * 3, [zout] * 2 + [yout] * 3
        scratch = []
        work = cost(4 * hd * k * j * rows, 5 * hd * k * rows + 2 * hd * k * j, 2 * hd * j * rows)
    return pl.pallas_call(
        body,
        grid_spec=pltpu.PrefetchScalarGridSpec(
            num_scalar_prefetch=1,
            grid=(hd // hb,),
            in_specs=in_specs,
            out_specs=out_specs,
            scratch_shapes=scratch,
        ),
        out_shape=out_shape,
        compiler_params=params(MIDDLE_MIB),
        cost_estimate=work,
        name="backward" if back else "forward",
    )(meta, *owns, *recvs, w2, w3, *saved)


def block_rows(own_ref, recv_ref, pa, hd, sub):
    wide = [ref[...].astype(F32) for ref in (own_ref, recv_ref)]
    rows = wide[0].shape[-1]
    return [
        jnp.concatenate(
            [v[:, a * sub : (a + 1) * sub, :].reshape(hd * sub, rows) for v in wide], axis=0
        ).astype(BF16)
        for a in range(pa)
    ]


def output_kernel(meta, zo_ref, zr_ref, w4_ref, out_ref, *, pa, bw, hd, sub):
    for a, z in enumerate(block_rows(zo_ref, zr_ref, pa, hd, sub)):
        out_ref[0, a * bw : (a + 1) * bw, :] = dot(w4_ref[0, 0, a], z, 0, 0).astype(BF16)


def output_parts(meta, z_own, z_recv, w14s, sub):
    same = w14s[0] is w14s[1]
    w4 = w14s[1]
    _, nl, wd, m2, bw = w4.shape
    hd, _, rows = z_own.shape
    pa = min(wd, 2)
    steps = wd // pa
    zspec = pl.BlockSpec((hd, pa * sub, rows), lambda k, s, meta: (0, k * steps + s, 0))
    wspec = pl.BlockSpec(
        (1, 1, pa, m2, bw), lambda k, s, meta: (1 if same else 0, meta[k], s, 0, 0)
    )
    return pl.pallas_call(
        functools.partial(output_kernel, pa=pa, bw=bw, hd=hd, sub=sub),
        grid_spec=pltpu.PrefetchScalarGridSpec(
            num_scalar_prefetch=1,
            grid=(nl, steps),
            in_specs=[zspec, zspec, wspec],
            out_specs=pl.BlockSpec((1, pa * bw, rows), lambda k, s, meta: (meta[k], s, 0)),
        ),
        out_shape=jax.ShapeDtypeStruct((nl, wd * bw, rows), BF16),
        compiler_params=params(16, 2),
        cost_estimate=cost(2 * nl * wd * m2 * bw * rows, nl * wd * (bw * rows + m2 * rows + m2 * bw)),
        name="output",
    )(meta, z_own, z_recv, w4)


def contract_kernel(meta, *refs, nx, late, chain, pa, bw, hd, sub, dp, scale):
    zo_ref, zr_ref, dyo_ref, dyr_ref, w1_ref = refs[:5]
    x_refs, g_refs = refs[5 : 5 + nx], refs[5 + nx : 5 + 2 * nx]
    refs = refs[5 + 2 * nx + (4 if chain else 0) :]
    part_ref, g1k_ref, g1s_ref, g4k_ref, g4s_ref, gsc = refs
    zs = block_rows(zo_ref, zr_ref, pa, hd, sub)
    dys = block_rows(dyo_ref, dyr_ref, pa, hd, sub)

    def shard(refs, span):
        if late:
            return jnp.where(meta[3] > 0, refs[1][span, :], refs[0][span, :])
        return total(refs, span)

    for a in range(pa):
        span = slice(a * bw, (a + 1) * bw)
        z, dy = zs[a], dys[a]
        part_ref[span, :] = dot(w1_ref[0, 0, a], dy, 1, 0).astype(BF16)
        g1 = dot(dy, shard(x_refs, span), 1, 1) * scale
        g4 = dot(z, shard(g_refs, span), 1, 1) * scale
        put_shares(meta, 4, gsc.at[a, 0], g1, g1k_ref, g1s_ref, (0, a), dp)
        put_shares(meta, 4 + dp, gsc.at[a, 1], g4, g4k_ref, g4s_ref, (0, a), dp)


def contract(k, meta, zdy, w14s, xs, gs, late, grads, sub, dp, scale):
    _, nl, wd, m2, bw = w14s[1].shape
    hd, _, rows = zdy[0].shape
    pa = min(wd, 2)
    steps = wd // pa
    half = dp // 2
    zspec = pl.BlockSpec((hd, pa * sub, rows), lambda s, meta: (0, k * steps + s, 0))
    xspec = pl.BlockSpec((pa * bw, rows), lambda s, meta: (s, 0))
    gspec = pl.BlockSpec((half, 1, pa, m2 // dp, bw), lambda s, meta: (0, meta[0], s, 0, 0))
    gout = jax.ShapeDtypeStruct((half, nl, wd, m2 // dp, bw), BF16)
    gtype = BF16 if (m2 // dp) % 16 == 0 else F32
    args = [meta, *zdy, w14s[0], *xs, *gs]
    specs = [zspec] * 4 + [weight_spec(0, w14s, pa)] + [xspec] * (2 * len(xs))
    aliases = {}
    if grads is not None:
        aliases = {len(args) + i: 1 + i for i in range(4)}
        args += list(grads)
        specs += [pl.BlockSpec(memory_space=pl.ANY)] * 4
    return pl.pallas_call(
        functools.partial(
            contract_kernel,
            nx=len(xs),
            late=late,
            chain=grads is not None,
            pa=pa,
            bw=bw,
            hd=hd,
            sub=sub,
            dp=dp,
            scale=scale,
        ),
        grid_spec=pltpu.PrefetchScalarGridSpec(
            num_scalar_prefetch=1,
            grid=(steps,),
            in_specs=specs,
            out_specs=[xspec, gspec, gspec, gspec, gspec],
            scratch_shapes=[pltpu.VMEM((pa, 2, m2, bw), gtype)],
        ),
        out_shape=[jax.ShapeDtypeStruct(xs[0].shape, BF16), gout, gout, gout, gout],
        input_output_aliases=aliases,
        compiler_params=params(20),
        cost_estimate=cost(
            6 * wd * m2 * bw * rows, wd * (3 * bw * rows + 2 * m2 * rows + 3 * m2 * bw)
        ),
        name="contract",
    )(*args)


def finish_kernel(tab, *refs, dp, piece, flip):
    val_refs, o_ref, sc = refs[:dp], refs[dp], refs[dp + 1]
    count = o_ref.shape[0]
    for a in range(count):
        for e in range(dp):
            val = val_refs[e][0, a].astype(F32)
            step = val.shape[0]
            share = lax.bitwise_xor(tab[0], e) * (step // piece)
            for i in range(step // piece):
                row = pl.multiple_of(tab[1 + share + i], piece)
                if flip:
                    sc[pl.ds(row, piece), :] = val[i * piece : (i + 1) * piece]
                else:
                    o_ref[a, pl.ds(row, piece), :] = val[i * piece : (i + 1) * piece]
        if flip:
            o_ref[a] = sc[...].T


def finish(tab, shares, flip):
    dp = len(shares)
    outer, wd, step, bw = shares[0].shape
    size = dp * step
    pieces = tab.shape[0] - 1
    piece = size // pieces
    count = min(wd, 8)
    if flip and size % 128:
        base = tab[0]
        merged = jnp.stack(shares)[jnp.arange(dp) ^ base]
        merged = jnp.transpose(merged, (1, 2, 0, 3, 4)).reshape(outer, wd, pieces, piece, bw)
        merged = merged[:, :, jnp.argsort(tab[1:])].reshape(outer, wd, size, bw)
        return jnp.transpose(merged, (1, 3, 0, 2)).reshape(wd, bw, outer * size).astype(F32)
    spec = pl.BlockSpec((1, count, step, bw), lambda o, a, tab: (o, a, 0, 0))
    if flip:
        shape = (wd, bw, outer * size)
        ospec = pl.BlockSpec((count, bw, size), lambda o, a, tab: (a, 0, o))
    else:
        shape = (wd, outer * size, bw)
        ospec = pl.BlockSpec((count, size, bw), lambda o, a, tab: (a, o, 0))
    return pl.pallas_call(
        functools.partial(finish_kernel, dp=dp, piece=piece, flip=flip),
        grid_spec=pltpu.PrefetchScalarGridSpec(
            num_scalar_prefetch=1,
            grid=(outer, wd // count),
            in_specs=[spec] * dp,
            out_specs=ospec,
            scratch_shapes=[pltpu.VMEM((size, bw), F32)],
        ),
        out_shape=jax.ShapeDtypeStruct(shape, F32),
        compiler_params=params(12, 2),
        cost_estimate=cost(0, 3 * wd * outer * size * bw),
        name="finish",
    )(tab, *shares)


def close_kernel(a_ref, b_ref, c_ref, out_ref):
    val = a_ref[...].astype(F32) + b_ref[...].astype(F32) + c_ref[...].astype(F32)
    out_ref[...] = val.T.astype(BF16)


def close(a, b, c):
    width, rows = a.shape
    block = min(width, 256)
    return pl.pallas_call(
        close_kernel,
        grid=(width // block,),
        in_specs=[pl.BlockSpec((block, rows), lambda s: (s, 0))] * 3,
        out_specs=pl.BlockSpec((rows, block), lambda s: (0, s)),
        out_shape=jax.ShapeDtypeStruct((rows, width), BF16),
        compiler_params=params(12),
        cost_estimate=cost(2 * width * rows, 4 * width * rows),
        name="close",
    )(a, b, c)


def up_pairs(lo, hi):
    return [(2 * p + c, 2 * p + 2 + c) for p in range(lo, hi) for c in range(2)]


def down_pairs(lo, hi):
    return [(2 * p + 2 + c, 2 * p + c) for p in range(lo, hi) for c in range(2)]


def swap(val, n):
    return lax.ppermute(val, "tensor", [(i, i ^ 1) for i in range(n)])


def add(a, b):
    return (a.astype(F32) + b.astype(F32)).astype(BF16)


X_PAIRS = [(i, i ^ 1) for i in range(4)]
Y_PAIRS = [(i, i ^ 2) for i in range(4)]


def reduce_dp(grads, dp, orders):
    if dp != 4:
        return [lax.psum_scatter(jnp.concatenate(pair), "dp") for pair in grads]
    came = [lax.ppermute(g[1], "dp", p[0]) for g, p in zip(grads, orders)]
    second = [add(g[0][1], c[1]) for g, c in zip(grads, came)]
    second = lax.optimization_barrier(second)
    second = [lax.ppermute(v, "dp", p[1]) for v, p in zip(second, orders)]
    return [
        (g[0][0].astype(F32) + c[0].astype(F32) + v.astype(F32)).astype(BF16)
        for g, c, v in zip(grads, came, second)
    ]


def gather_dp(val, dp, x_last):
    if dp != 4:
        every = lax.all_gather(val, "dp")
        return [every[q] for q in range(dp)]
    by_x = lax.ppermute(val, "dp", X_PAIRS)
    by_y = lax.ppermute(val, "dp", Y_PAIRS)
    if x_last:
        diag = lax.ppermute(by_y, "dp", X_PAIRS)
    else:
        diag = lax.ppermute(by_x, "dp", Y_PAIRS)
    return [val, by_x, by_y, diag]


def body(tokens, cotangent, w_first, w_second, w_third, w_fourth):
    rows = tokens.shape[0]
    wd, bw, _ = w_first.shape
    hd = w_second.shape[0]
    n = lax.axis_size("tensor")
    dp = lax.axis_size("dp")
    nl = n // 2
    sub = bw // (wd * n)
    part = wd * sub
    m = hd * sub
    m2 = 2 * m
    step = m2 // dp
    scale = 1.0 / math.sqrt(rows * dp)
    me = lax.axis_index("tensor")
    mine = lax.axis_index("dp")
    pos, core = me // 2, me % 2
    lines = [[2 * p + c for p in range(nl)] for c in range(2)]
    x_first, y_first = (X_PAIRS, Y_PAIRS), (Y_PAIRS, X_PAIRS)

    dps = jnp.arange(dp, dtype=jnp.int32)
    if dp == 4:
        inv_x = (((dps & 1) << 1) | (dps >> 1)) ^ mine
        inv_y = dps ^ mine
        base = mine
    else:
        inv_x = inv_y = dps
        base = mine * 0
    low_end, high_end = pos == 0, pos == nl - 1
    late_slot = jnp.where(low_end, nl - 1, jnp.where(high_end, 1, -1))

    def meta_of(head, late):
        head = jnp.stack([jnp.asarray(v, jnp.int32) for v in (head, core, late_slot, late)])
        return jnp.concatenate([head, inv_x, inv_y])

    w1 = lax.dynamic_index_in_dim(
        w_first.reshape(wd, dp, bw // dp, nl * m2), mine, axis=1, keepdims=False
    )
    w4 = lax.dynamic_index_in_dim(
        w_fourth.reshape(wd, nl, dp, step, bw), mine, axis=2, keepdims=False
    )
    if m2 == bw:
        w1 = w1.reshape(wd, step, nl, bw)
        w14 = jnp.stack([jnp.transpose(w1, (2, 0, 1, 3)), jnp.transpose(w4, (1, 0, 2, 3))], axis=1)
        w14 = lax.all_to_all(
            w14, "tensor", split_axis=0, concat_axis=0, axis_index_groups=lines, tiled=True
        )
        sides = [w14[:, 0], w14[:, 1]]
    else:
        w1 = jnp.transpose(w1.reshape(wd, bw // dp, nl, m2), (2, 0, 1, 3))
        w4 = jnp.transpose(w4, (1, 0, 2, 3))
        sides = [
            lax.all_to_all(
                w, "tensor", split_axis=0, concat_axis=0, axis_index_groups=lines, tiled=True
            )
            for w in (w1, w4)
        ]
    x_own, g_own = tokens.T, cotangent.T
    x_own, sides = lax.optimization_barrier((x_own, sides))
    whole = dp == 4 and m2 == bw
    if whole:
        by_x = lax.ppermute(w14, "dp", X_PAIRS)
        by_y = lax.ppermute(w14, "dp", Y_PAIRS)
        gate = [by_x, by_y]
    else:
        gate = [lax.all_gather(w, "dp") for w in sides]

    def relative(w):
        w = w.reshape(hd, nl, 2, part, bw)
        w = jnp.where(core == 0, w, w[:, :, ::-1])
        w = lax.dynamic_slice_in_dim(jnp.concatenate([w, w], axis=1), pos, nl, axis=1)
        return w.reshape(hd, bw, bw)

    w2 = relative(w_second)
    w3 = relative(jnp.swapaxes(w_third, 1, 2))

    def hop(ups, downs, r):
        up = lax.ppermute(ups[-1], "tensor", up_pairs(r - 1, nl - 1))
        down = lax.ppermute(downs[-1], "tensor", down_pairs(0, nl - r))
        return up, down

    x_ups, x_downs = [x_own], [x_own]
    for r in range(1, nl):
        up, down = hop(x_ups, x_downs, r)
        if r == 1:
            up, down, gate, w2, w3 = lax.optimization_barrier((up, down, gate, w2, w3))
            if whole:
                by_x, by_y = gate
                gate = [
                    lax.ppermute(by_y[:, 0], "dp", X_PAIRS),
                    lax.ppermute(by_x[:, 1], "dp", Y_PAIRS),
                ]
        elif r == 2:
            up, down, gate, g_own = lax.optimization_barrier((up, down, gate, g_own))
        x_ups.append(up)
        x_downs.append(down)
    g_ups, g_downs = [g_own], [g_own]
    for r in range(1, nl):
        up, down = hop(g_ups, g_downs, r)
        up, down = lax.optimization_barrier((up, down))
        g_ups.append(up)
        g_downs.append(down)
    if whole:
        w14s = (assemble(core, mine, w14, by_x, by_y, gate),) * 2
    else:
        w1, w4 = gate
        w1 = jnp.transpose(w1, (1, 2, 0, 3, 4)).reshape(nl, wd, bw, 2, m)
        w4 = jnp.transpose(w4, (1, 2, 0, 3, 4)).reshape(nl, wd, 2, m, bw)
        w1 = jnp.where(core == 0, w1, w1[:, :, :, ::-1]).reshape(nl, wd, bw, m2)
        w4 = jnp.where(core == 0, w4, w4[:, :, ::-1]).reshape(nl, wd, m2, bw)
        w14s = (w1[None], w4[None])

    def slots_of(ups, downs):
        slots = [[ups[0]], [downs[1]]]
        slots += [[downs[k], ups[nl - k]] for k in range(2, nl - 1)]
        return slots + [[ups[1]], [ups[nl - 1], downs[nl - 1]]]

    metas = [meta_of((pos + k) % nl, 0) for k in range(nl)]
    metas[1] = meta_of((pos + 1) % nl, high_end)
    metas[nl - 1] = meta_of((pos + nl - 1) % nl, low_end)
    metas.append(meta_of(jnp.where(low_end, nl - 1, 0), 0))

    def first_factor(side, slots):
        owns, recvs = [], []
        for meta, xs in zip(metas, slots):
            mine_part, send = expand(side, meta, xs, w14s, hd, sub)
            owns.append(mine_part)
            recvs.append(swap(send, n))
        return owns, recvs

    x_slots, g_slots = slots_of(x_ups, x_downs), slots_of(g_ups, g_downs)
    owns, recvs = first_factor(0, x_slots)
    z_own, z_send, *saved = middle(False, metas[0], owns, recvs, w2, w3, [], dp, scale)
    z_recv = swap(z_send, n)
    places = ((pos + jnp.arange(nl)) % nl).astype(jnp.int32)
    outs = output_parts(places, z_own, z_recv, w14s, sub)
    layer_out = lax.psum_scatter(outs, "tensor", axis_index_groups=lines).T

    owns, recvs = first_factor(1, g_slots)
    dy_own, dy_send, *g23 = middle(True, metas[0], owns, recvs, w2, w3, saved, dp, scale)
    dy_recv = swap(dy_send, n)
    parts, grads = [None] * nl, None
    order = [k for pair in zip(range(nl - 1, nl // 2, -1), range(1, nl // 2)) for k in pair]
    for k in order + [nl // 2, 0]:
        late = k in (1, nl - 1)
        xs, gs = x_slots[k], g_slots[k]
        if late:
            xs = xs + [x_slots[nl][0 if k == 1 else 1]]
            gs = gs + [g_slots[nl][0 if k == 1 else 1]]
        parts[k], *grads = contract(
            k,
            metas[k],
            (z_own, z_recv, dy_own, dy_recv),
            w14s,
            xs,
            gs,
            late,
            grads,
            sub,
            dp,
            scale,
        )

    g1, g2, g3, g4 = reduce_dp(
        [grads[:2], g23[:2], g23[2:], grads[2:]], dp, (x_first, x_first, y_first, y_first)
    )
    g14 = jnp.stack([g1, g4], axis=1)
    g14 = lax.all_to_all(
        g14, "tensor", split_axis=0, concat_axis=0, axis_index_groups=lines, tiled=True
    )

    up, down = parts[nl - 1], parts[1]
    for r in range(1, nl):
        if r == nl - 1:
            up, down, g14 = lax.optimization_barrier((up, down, g14))
        up = lax.ppermute(up, "tensor", up_pairs(0, r))
        down = lax.ppermute(down, "tensor", down_pairs(nl - 1 - r, nl - 1))
        if r < nl - 1:
            up = add(up, parts[nl - 1 - r])
            down = add(down, parts[r + 1])
            up, down = lax.optimization_barrier((up, down))

    g2 = gather_dp(g2, dp, True)
    g3 = gather_dp(g3, dp, False)
    g1 = gather_dp(g14[:, 0], dp, True)
    g4 = gather_dp(g14[:, 1], dp, False)
    tokens_grad = close(parts[0], up, down)

    base = jnp.asarray(base, jnp.int32)[None]
    offset = jnp.arange(2 * nl, dtype=jnp.int32)
    wide_rows = (((offset // 2 + pos) % nl) * 2 + (offset + core) % 2) * part
    dual_rows = (jnp.arange(dp, dtype=jnp.int32) * step + core * m) % m2
    wide_tab = jnp.concatenate([base, wide_rows.astype(jnp.int32)])
    dual_tab = jnp.concatenate([base, dual_rows.astype(jnp.int32)])
    out_two = finish(wide_tab, [g[None] for g in g2], False)
    out_three = finish(wide_tab, [g[None] for g in g3], True)
    g1, g4, out_two, out_three = lax.optimization_barrier((g1, g4, out_two, out_three))
    return (
        layer_out,
        tokens_grad,
        finish(dual_tab, g1, True),
        out_two,
        out_three,
        finish(dual_tab, g4, False),
    )


def solution(mesh):
    return jax.shard_map(
        body,
        mesh=mesh,
        in_specs=(
            P("dp", "tensor"),
            P("dp", "tensor"),
            P("tensor", None, None),
            P("tensor", None, None),
            P("tensor", None, None),
            P("tensor", None, None),
        ),
        out_specs=(
            P("dp", "tensor"),
            P("dp", "tensor"),
            P("tensor", None, None),
            P("tensor", None, None),
            P("tensor", None, None),
            P("tensor", None, None),
        ),
        check_vma=False,
    )
```

```python
import functools
import math

import jax
import jax.numpy as jnp
from jax import lax
from jax.experimental import pallas as pl
from jax.experimental.pallas import tpu as pltpu
from jax.sharding import PartitionSpec as P

F32 = jnp.float32
BF16 = jnp.bfloat16
MIDDLE_MIB = 40


def params(mib, dims=1):
    return pltpu.CompilerParams(
        dimension_semantics=("arbitrary",) * dims, vmem_limit_bytes=mib * 1024 * 1024
    )


def gelu_parts(value_in):
    cdf_part = 0.5 * (1.0 + lax.erf(value_in * 0.7071067811865476))
    slope_part = cdf_part + value_in * jnp.exp(-0.5 * value_in * value_in) * 0.3989422804014327
    return (value_in * cdf_part, slope_part)


def dot(a, b, ca, cb):
    return lax.dot_general(a, b, (((ca,), (cb,)), ((), ())), preferred_element_type=F32)


def cost(flops, elements, trans=0):
    return pl.CostEstimate(flops=flops, bytes_accessed=2 * elements, transcendentals=trans)


def assemble_kernel(meta, *refs):
    out_ref = refs[-1]
    _, _, wd, size, bw = out_ref.shape
    step = size // 4
    half = size // 2
    low = meta[0] == 0
    for e in range(4):
        share = lax.bitwise_xor(meta[1], e) * step
        first = refs[e][0, 0] if e < 3 else refs[3][0]
        second = refs[e][0, 1] if e < 3 else refs[4][0]
        left, right = first[:, :, : bw // 2], first[:, :, bw // 2 :]
        first = jnp.concatenate(
            [jnp.where(low, left, right), jnp.where(low, right, left)], axis=2
        )
        out_ref[0, 0, :, pl.ds(pl.multiple_of(share, step), step), :] = first
        row = lax.rem(share + meta[0] * half, size)
        out_ref[1, 0, :, pl.ds(pl.multiple_of(row, step), step), :] = second


def assemble(core, mine, own, by_x, by_y, diag):
    nl, _, wd, step, bw = own.shape
    spec = pl.BlockSpec((1, 2, wd, step, bw), lambda k, meta: (k, 0, 0, 0, 0))
    dspec = pl.BlockSpec((1, wd, step, bw), lambda k, meta: (k, 0, 0, 0))
    return pl.pallas_call(
        assemble_kernel,
        grid_spec=pltpu.PrefetchScalarGridSpec(
            num_scalar_prefetch=1,
            grid=(nl,),
            in_specs=[spec, spec, spec, dspec, dspec],
            out_specs=pl.BlockSpec((2, 1, wd, 4 * step, bw), lambda k, meta: (0, k, 0, 0, 0)),
        ),
        out_shape=jax.ShapeDtypeStruct((2, nl, wd, 4 * step, bw), BF16),
        compiler_params=params(12),
        cost_estimate=cost(0, 16 * nl * wd * step * bw),
        name="assemble",
    )(jnp.stack([core, mine]).astype(jnp.int32), own, by_x, by_y, *diag)


def total(refs, span):
    val = refs[0][span, :]
    for ref in refs[1:]:
        val = val + ref[span, :]
    return val


def weight_spec(side, w14s, pa):
    same = w14s[0] is w14s[1]
    shape = (1, 1, pa, *w14s[side].shape[3:])
    return pl.BlockSpec(shape, lambda s, meta: (side if same else 0, meta[0], s, 0, 0))


def expand_kernel(meta, *refs, side, pa, bw, hd, sub):
    x_refs, (w_ref, own_ref, send_ref) = refs[:-3], refs[-3:]
    m = hd * sub
    own, send = [], []
    for a in range(pa):
        x = total(x_refs, slice(a * bw, (a + 1) * bw))
        val = dot(w_ref[0, 0, a], x, side, 0)
        own.append(val[:m].reshape(hd, sub, val.shape[-1]))
        send.append(val[m:].reshape(hd, sub, val.shape[-1]))
    own_ref[...] = jnp.concatenate(own, axis=1).astype(BF16)
    send_ref[...] = jnp.concatenate(send, axis=1).astype(BF16)


def expand(side, meta, xs, w14s, hd, sub):
    _, nl, wd, m2, bw = w14s[1].shape
    rows = xs[0].shape[-1]
    pa = min(wd, 2)
    out = jax.ShapeDtypeStruct((hd, wd * sub, rows), BF16)
    out_spec = pl.BlockSpec((hd, pa * sub, rows), lambda s, meta: (0, s, 0))
    return pl.pallas_call(
        functools.partial(expand_kernel, side=side, pa=pa, bw=bw, hd=hd, sub=sub),
        grid_spec=pltpu.PrefetchScalarGridSpec(
            num_scalar_prefetch=1,
            grid=(wd // pa,),
            in_specs=[pl.BlockSpec((pa * bw, rows), lambda s, meta: (s, 0))] * len(xs)
            + [weight_spec(side, w14s, pa)],
            out_specs=[out_spec, out_spec],
        ),
        out_shape=[out, out],
        compiler_params=params(12),
        cost_estimate=cost(2 * wd * m2 * bw * rows, wd * (bw * rows + m2 * bw + m2 * rows)),
        name="expand",
    )(meta, *xs, w14s[side])


def put_shares(meta, first, gsc, val, keep_ref, send_ref, index, dp):
    step = val.shape[0] // dp
    gsc[...] = val.astype(gsc.dtype)
    half = dp // 2
    for p in range(dp):
        row = pl.multiple_of(meta[first + p] * step, step)
        ref = keep_ref if p < half else send_ref
        ref[(p % half, *index)] = gsc[pl.ds(row, step), :].astype(BF16)


def join(pieces):
    if pieces[0].shape[0] % 16:
        return jnp.concatenate([p.astype(F32) for p in pieces], axis=0).astype(BF16)
    return jnp.concatenate(pieces, axis=0)


def rows_of(meta, sides, b, nl):
    pieces = []
    for k in range(nl):
        for side in sides:
            val = side[k][b]
            if k in (1, nl - 1):
                val = jnp.where(meta[2] == k, side[nl][b], val)
            pieces.append(val)
    return join(pieces)


def split_cores(val, own_ref, send_ref, b, nl, part):
    for k in range(nl):
        own_ref[b, k * part : (k + 1) * part] = val[2 * k * part : (2 * k + 1) * part].astype(BF16)
        send_ref[b, k * part : (k + 1) * part] = val[(2 * k + 1) * part : (2 * k + 2) * part].astype(BF16)


def forward_kernel(meta, *refs, nl, part, hb):
    sides = (refs[: nl + 1], refs[nl + 1 : 2 * nl + 2])
    w2_ref, w3_ref, own_ref, send_ref, y_ref, act_ref, slope_ref = refs[2 * nl + 2 :]
    for b in range(hb):
        yb = rows_of(meta, sides, b, nl)
        y_ref[b] = yb
        val, slope = gelu_parts(dot(w2_ref[b], yb, 0, 0))
        act = val.astype(BF16)
        act_ref[b] = act
        slope_ref[b] = slope.astype(BF16)
        split_cores(dot(w3_ref[b], act, 1, 0), own_ref, send_ref, b, nl, part)


def backward_kernel(meta, *refs, nl, part, hb, dp, scale):
    sides = (refs[: nl + 1], refs[nl + 1 : 2 * nl + 2])
    refs = refs[2 * nl + 2 :]
    w2_ref, w3_ref, y_ref, act_ref, slope_ref, own_ref, send_ref = refs[:7]
    g2k_ref, g2s_ref, g3k_ref, g3s_ref, gsc = refs[7:]
    for b in range(hb):
        dzb = rows_of(meta, sides, b, nl)
        dact = dot(w3_ref[b], dzb, 0, 0)
        dpre = (dact * slope_ref[b].astype(F32)).astype(BF16)
        split_cores(dot(w2_ref[b], dpre, 1, 0), own_ref, send_ref, b, nl, part)
        put_shares(meta, 4, gsc.at[b, 0], dot(y_ref[b], dpre, 1, 1) * scale, g2k_ref, g2s_ref, (b,), dp)
        put_shares(
            meta, 4 + dp, gsc.at[b, 1], dot(dzb, act_ref[b], 1, 1) * scale, g3k_ref, g3s_ref, (b,), dp
        )


def middle(back, meta, owns, recvs, w2, w3, saved, dp, scale):
    hd, k, j = w2.shape
    nl = len(owns) - 1
    _, part, rows = owns[0].shape
    hb = 4
    half = dp // 2
    slot = pl.BlockSpec((hb, part, rows), lambda b, meta: (b, 0, 0))
    one = pl.BlockSpec((hb, nl * part, rows), lambda b, meta: (b, 0, 0))
    full = pl.BlockSpec((hb, k, rows), lambda b, meta: (b, 0, 0))
    wspec = pl.BlockSpec((hb, k, j), lambda b, meta: (b, 0, 0))
    gspec = pl.BlockSpec((half, hb, k // dp, j), lambda b, meta: (0, b, 0, 0))
    zout = jax.ShapeDtypeStruct((hd, nl * part, rows), BF16)
    yout = jax.ShapeDtypeStruct((hd, k, rows), BF16)
    gout = jax.ShapeDtypeStruct((half, hd, k // dp, j), BF16)
    gtype = BF16 if (k // dp) % 16 == 0 else F32
    in_specs = [slot] * (2 * nl + 2) + [wspec, wspec]
    if back:
        body = functools.partial(backward_kernel, nl=nl, part=part, hb=hb, dp=dp, scale=scale)
        in_specs += [full] * 3
        out_specs, out_shape = [one] * 2 + [gspec] * 4, [zout] * 2 + [gout] * 4
        scratch = [pltpu.VMEM((hb, 2, k, j), gtype)]
        work = cost(8 * hd * k * j * rows, 5 * hd * k * rows + 4 * hd * k * j)
    else:
        body = functools.partial(forward_kernel, nl=nl, part=part, hb=hb)
        out_specs, out_shape = [one] * 2 + [full] * 3, [zout] * 2 + [yout] * 3
        scratch = []
        work = cost(4 * hd * k * j * rows, 5 * hd * k * rows + 2 * hd * k * j, 2 * hd * j * rows)
    return pl.pallas_call(
        body,
        grid_spec=pltpu.PrefetchScalarGridSpec(
            num_scalar_prefetch=1,
            grid=(hd // hb,),
            in_specs=in_specs,
            out_specs=out_specs,
            scratch_shapes=scratch,
        ),
        out_shape=out_shape,
        compiler_params=params(MIDDLE_MIB),
        cost_estimate=work,
        name="backward" if back else "forward",
    )(meta, *owns, *recvs, w2, w3, *saved)


def block_rows(own_ref, recv_ref, pa, hd, sub):
    wide = [ref[...].astype(F32) for ref in (own_ref, recv_ref)]
    rows = wide[0].shape[-1]
    return [
        jnp.concatenate(
            [v[:, a * sub : (a + 1) * sub, :].reshape(hd * sub, rows) for v in wide], axis=0
        ).astype(BF16)
        for a in range(pa)
    ]


def output_kernel(meta, zo_ref, zr_ref, w4_ref, out_ref, *, pa, bw, hd, sub):
    for a, z in enumerate(block_rows(zo_ref, zr_ref, pa, hd, sub)):
        out_ref[0, a * bw : (a + 1) * bw, :] = dot(w4_ref[0, 0, a], z, 0, 0).astype(BF16)


def output_parts(meta, z_own, z_recv, w14s, sub):
    same = w14s[0] is w14s[1]
    w4 = w14s[1]
    _, nl, wd, m2, bw = w4.shape
    hd, _, rows = z_own.shape
    pa = min(wd, 2)
    steps = wd // pa
    zspec = pl.BlockSpec((hd, pa * sub, rows), lambda k, s, meta: (0, k * steps + s, 0))
    wspec = pl.BlockSpec(
        (1, 1, pa, m2, bw), lambda k, s, meta: (1 if same else 0, meta[k], s, 0, 0)
    )
    return pl.pallas_call(
        functools.partial(output_kernel, pa=pa, bw=bw, hd=hd, sub=sub),
        grid_spec=pltpu.PrefetchScalarGridSpec(
            num_scalar_prefetch=1,
            grid=(nl, steps),
            in_specs=[zspec, zspec, wspec],
            out_specs=pl.BlockSpec((1, pa * bw, rows), lambda k, s, meta: (meta[k], s, 0)),
        ),
        out_shape=jax.ShapeDtypeStruct((nl, wd * bw, rows), BF16),
        compiler_params=params(16, 2),
        cost_estimate=cost(2 * nl * wd * m2 * bw * rows, nl * wd * (bw * rows + m2 * rows + m2 * bw)),
        name="output",
    )(meta, z_own, z_recv, w4)


def contract_kernel(meta, *refs, nx, late, chain, pa, bw, hd, sub, dp, scale):
    zo_ref, zr_ref, dyo_ref, dyr_ref, w1_ref = refs[:5]
    x_refs, g_refs = refs[5 : 5 + nx], refs[5 + nx : 5 + 2 * nx]
    refs = refs[5 + 2 * nx + (4 if chain else 0) :]
    part_ref, g1k_ref, g1s_ref, g4k_ref, g4s_ref, gsc = refs
    zs = block_rows(zo_ref, zr_ref, pa, hd, sub)
    dys = block_rows(dyo_ref, dyr_ref, pa, hd, sub)

    def shard(refs, span):
        if late:
            return jnp.where(meta[3] > 0, refs[1][span, :], refs[0][span, :])
        return total(refs, span)

    for a in range(pa):
        span = slice(a * bw, (a + 1) * bw)
        z, dy = zs[a], dys[a]
        part_ref[span, :] = dot(w1_ref[0, 0, a], dy, 1, 0).astype(BF16)
        g1 = dot(dy, shard(x_refs, span), 1, 1) * scale
        g4 = dot(z, shard(g_refs, span), 1, 1) * scale
        put_shares(meta, 4, gsc.at[a, 0], g1, g1k_ref, g1s_ref, (0, a), dp)
        put_shares(meta, 4 + dp, gsc.at[a, 1], g4, g4k_ref, g4s_ref, (0, a), dp)


def contract(k, meta, zdy, w14s, xs, gs, late, grads, sub, dp, scale):
    _, nl, wd, m2, bw = w14s[1].shape
    hd, _, rows = zdy[0].shape
    pa = min(wd, 2)
    steps = wd // pa
    half = dp // 2
    zspec = pl.BlockSpec((hd, pa * sub, rows), lambda s, meta: (0, k * steps + s, 0))
    xspec = pl.BlockSpec((pa * bw, rows), lambda s, meta: (s, 0))
    gspec = pl.BlockSpec((half, 1, pa, m2 // dp, bw), lambda s, meta: (0, meta[0], s, 0, 0))
    gout = jax.ShapeDtypeStruct((half, nl, wd, m2 // dp, bw), BF16)
    gtype = BF16 if (m2 // dp) % 16 == 0 else F32
    args = [meta, *zdy, w14s[0], *xs, *gs]
    specs = [zspec] * 4 + [weight_spec(0, w14s, pa)] + [xspec] * (2 * len(xs))
    aliases = {}
    if grads is not None:
        aliases = {len(args) + i: 1 + i for i in range(4)}
        args += list(grads)
        specs += [pl.BlockSpec(memory_space=pl.ANY)] * 4
    return pl.pallas_call(
        functools.partial(
            contract_kernel,
            nx=len(xs),
            late=late,
            chain=grads is not None,
            pa=pa,
            bw=bw,
            hd=hd,
            sub=sub,
            dp=dp,
            scale=scale,
        ),
        grid_spec=pltpu.PrefetchScalarGridSpec(
            num_scalar_prefetch=1,
            grid=(steps,),
            in_specs=specs,
            out_specs=[xspec, gspec, gspec, gspec, gspec],
            scratch_shapes=[pltpu.VMEM((pa, 2, m2, bw), gtype)],
        ),
        out_shape=[jax.ShapeDtypeStruct(xs[0].shape, BF16), gout, gout, gout, gout],
        input_output_aliases=aliases,
        compiler_params=params(20),
        cost_estimate=cost(
            6 * wd * m2 * bw * rows, wd * (3 * bw * rows + 2 * m2 * rows + 3 * m2 * bw)
        ),
        name="contract",
    )(*args)


def finish_kernel(tab, *refs, dp, piece, flip):
    val_refs, o_ref, sc = refs[:dp], refs[dp], refs[dp + 1]
    count = o_ref.shape[0]
    for a in range(count):
        for e in range(dp):
            val = val_refs[e][0, a].astype(F32)
            step = val.shape[0]
            share = lax.bitwise_xor(tab[0], e) * (step // piece)
            for i in range(step // piece):
                row = pl.multiple_of(tab[1 + share + i], piece)
                if flip:
                    sc[pl.ds(row, piece), :] = val[i * piece : (i + 1) * piece]
                else:
                    o_ref[a, pl.ds(row, piece), :] = val[i * piece : (i + 1) * piece]
        if flip:
            o_ref[a] = sc[...].T


def finish(tab, shares, flip):
    dp = len(shares)
    outer, wd, step, bw = shares[0].shape
    size = dp * step
    pieces = tab.shape[0] - 1
    piece = size // pieces
    count = min(wd, 8)
    if flip and size % 128:
        base = tab[0]
        merged = jnp.stack(shares)[jnp.arange(dp) ^ base]
        merged = jnp.transpose(merged, (1, 2, 0, 3, 4)).reshape(outer, wd, pieces, piece, bw)
        merged = merged[:, :, jnp.argsort(tab[1:])].reshape(outer, wd, size, bw)
        return jnp.transpose(merged, (1, 3, 0, 2)).reshape(wd, bw, outer * size).astype(F32)
    spec = pl.BlockSpec((1, count, step, bw), lambda o, a, tab: (o, a, 0, 0))
    if flip:
        shape = (wd, bw, outer * size)
        ospec = pl.BlockSpec((count, bw, size), lambda o, a, tab: (a, 0, o))
    else:
        shape = (wd, outer * size, bw)
        ospec = pl.BlockSpec((count, size, bw), lambda o, a, tab: (a, o, 0))
    return pl.pallas_call(
        functools.partial(finish_kernel, dp=dp, piece=piece, flip=flip),
        grid_spec=pltpu.PrefetchScalarGridSpec(
            num_scalar_prefetch=1,
            grid=(outer, wd // count),
            in_specs=[spec] * dp,
            out_specs=ospec,
            scratch_shapes=[pltpu.VMEM((size, bw), F32)],
        ),
        out_shape=jax.ShapeDtypeStruct(shape, F32),
        compiler_params=params(12, 2),
        cost_estimate=cost(0, 3 * wd * outer * size * bw),
        name="finish",
    )(tab, *shares)


def close_kernel(a_ref, b_ref, c_ref, out_ref):
    val = a_ref[...].astype(F32) + b_ref[...].astype(F32) + c_ref[...].astype(F32)
    out_ref[...] = val.T.astype(BF16)


def close(a, b, c):
    width, rows = a.shape
    block = min(width, 256)
    return pl.pallas_call(
        close_kernel,
        grid=(width // block,),
        in_specs=[pl.BlockSpec((block, rows), lambda s: (s, 0))] * 3,
        out_specs=pl.BlockSpec((rows, block), lambda s: (0, s)),
        out_shape=jax.ShapeDtypeStruct((rows, width), BF16),
        compiler_params=params(12),
        cost_estimate=cost(2 * width * rows, 4 * width * rows),
        name="close",
    )(a, b, c)


def up_pairs(lo, hi):
    return [(2 * p + c, 2 * p + 2 + c) for p in range(lo, hi) for c in range(2)]


def down_pairs(lo, hi):
    return [(2 * p + 2 + c, 2 * p + c) for p in range(lo, hi) for c in range(2)]


def swap(val, n):
    return lax.ppermute(val, "tensor", [(i, i ^ 1) for i in range(n)])


def add(a, b):
    return (a.astype(F32) + b.astype(F32)).astype(BF16)


X_PAIRS = [(i, i ^ 1) for i in range(4)]
Y_PAIRS = [(i, i ^ 2) for i in range(4)]


def reduce_dp(grads, dp, orders):
    if dp != 4:
        return [lax.psum_scatter(jnp.concatenate(pair), "dp") for pair in grads]
    came = [lax.ppermute(g[1], "dp", p[0]) for g, p in zip(grads, orders)]
    second = [add(g[0][1], c[1]) for g, c in zip(grads, came)]
    second = lax.optimization_barrier(second)
    second = [lax.ppermute(v, "dp", p[1]) for v, p in zip(second, orders)]
    return [
        (g[0][0].astype(F32) + c[0].astype(F32) + v.astype(F32)).astype(BF16)
        for g, c, v in zip(grads, came, second)
    ]


def gather_dp(val, dp, x_last):
    if dp != 4:
        every = lax.all_gather(val, "dp")
        return [every[q] for q in range(dp)]
    by_x = lax.ppermute(val, "dp", X_PAIRS)
    by_y = lax.ppermute(val, "dp", Y_PAIRS)
    if x_last:
        diag = lax.ppermute(by_y, "dp", X_PAIRS)
    else:
        diag = lax.ppermute(by_x, "dp", Y_PAIRS)
    return [val, by_x, by_y, diag]


def body(tokens, cotangent, w_first, w_second, w_third, w_fourth):
    rows = tokens.shape[0]
    wd, bw, _ = w_first.shape
    hd = w_second.shape[0]
    n = lax.axis_size("tensor")
    dp = lax.axis_size("dp")
    nl = n // 2
    sub = bw // (wd * n)
    part = wd * sub
    m = hd * sub
    m2 = 2 * m
    step = m2 // dp
    scale = 1.0 / math.sqrt(rows * dp)
    me = lax.axis_index("tensor")
    mine = lax.axis_index("dp")
    pos, core = me // 2, me % 2
    lines = [[2 * p + c for p in range(nl)] for c in range(2)]
    x_first, y_first = (X_PAIRS, Y_PAIRS), (Y_PAIRS, X_PAIRS)

    dps = jnp.arange(dp, dtype=jnp.int32)
    if dp == 4:
        inv_x = (((dps & 1) << 1) | (dps >> 1)) ^ mine
        inv_y = dps ^ mine
        base = mine
    else:
        inv_x = inv_y = dps
        base = mine * 0
    low_end, high_end = pos == 0, pos == nl - 1
    late_slot = jnp.where(low_end, nl - 1, jnp.where(high_end, 1, -1))

    def meta_of(head, late):
        head = jnp.stack([jnp.asarray(v, jnp.int32) for v in (head, core, late_slot, late)])
        return jnp.concatenate([head, inv_x, inv_y])

    w1 = lax.dynamic_index_in_dim(
        w_first.reshape(wd, dp, bw // dp, nl * m2), mine, axis=1, keepdims=False
    )
    w4 = lax.dynamic_index_in_dim(
        w_fourth.reshape(wd, nl, dp, step, bw), mine, axis=2, keepdims=False
    )
    if m2 == bw:
        w1 = w1.reshape(wd, step, nl, bw)
        w14 = jnp.stack([jnp.transpose(w1, (2, 0, 1, 3)), jnp.transpose(w4, (1, 0, 2, 3))], axis=1)
        w14 = lax.all_to_all(
            w14, "tensor", split_axis=0, concat_axis=0, axis_index_groups=lines, tiled=True
        )
        sides = [w14[:, 0], w14[:, 1]]
    else:
        w1 = jnp.transpose(w1.reshape(wd, bw // dp, nl, m2), (2, 0, 1, 3))
        w4 = jnp.transpose(w4, (1, 0, 2, 3))
        sides = [
            lax.all_to_all(
                w, "tensor", split_axis=0, concat_axis=0, axis_index_groups=lines, tiled=True
            )
            for w in (w1, w4)
        ]
    x_own, g_own = tokens.T, cotangent.T
    x_own, sides = lax.optimization_barrier((x_own, sides))
    whole = dp == 4 and m2 == bw
    if whole:
        by_x = lax.ppermute(w14, "dp", X_PAIRS)
        by_y = lax.ppermute(w14, "dp", Y_PAIRS)
        gate = [by_x, by_y]
    else:
        gate = [lax.all_gather(w, "dp") for w in sides]

    def relative(w):
        w = w.reshape(hd, nl, 2, part, bw)
        w = jnp.where(core == 0, w, w[:, :, ::-1])
        w = lax.dynamic_slice_in_dim(jnp.concatenate([w, w], axis=1), pos, nl, axis=1)
        return w.reshape(hd, bw, bw)

    w2 = relative(w_second)
    w3 = relative(jnp.swapaxes(w_third, 1, 2))

    def hop(ups, downs, r):
        up = lax.ppermute(ups[-1], "tensor", up_pairs(r - 1, nl - 1))
        down = lax.ppermute(downs[-1], "tensor", down_pairs(0, nl - r))
        return up, down

    x_ups, x_downs = [x_own], [x_own]
    for r in range(1, nl):
        up, down = hop(x_ups, x_downs, r)
        if r == 1:
            up, down, gate, w2, w3 = lax.optimization_barrier((up, down, gate, w2, w3))
            if whole:
                by_x, by_y = gate
                gate = [
                    lax.ppermute(by_y[:, 0], "dp", X_PAIRS),
                    lax.ppermute(by_x[:, 1], "dp", Y_PAIRS),
                ]
        elif r == 2:
            up, down, gate, g_own = lax.optimization_barrier((up, down, gate, g_own))
        x_ups.append(up)
        x_downs.append(down)
    g_ups, g_downs = [g_own], [g_own]
    for r in range(1, nl):
        up, down = hop(g_ups, g_downs, r)
        up, down = lax.optimization_barrier((up, down))
        g_ups.append(up)
        g_downs.append(down)
    if whole:
        w14s = (assemble(core, mine, w14, by_x, by_y, gate),) * 2
    else:
        w1, w4 = gate
        w1 = jnp.transpose(w1, (1, 2, 0, 3, 4)).reshape(nl, wd, bw, 2, m)
        w4 = jnp.transpose(w4, (1, 2, 0, 3, 4)).reshape(nl, wd, 2, m, bw)
        w1 = jnp.where(core == 0, w1, w1[:, :, :, ::-1]).reshape(nl, wd, bw, m2)
        w4 = jnp.where(core == 0, w4, w4[:, :, ::-1]).reshape(nl, wd, m2, bw)
        w14s = (w1[None], w4[None])

    def slots_of(ups, downs):
        slots = [[ups[0]], [downs[1]]]
        slots += [[downs[k], ups[nl - k]] for k in range(2, nl - 1)]
        return slots + [[ups[1]], [ups[nl - 1], downs[nl - 1]]]

    metas = [meta_of((pos + k) % nl, 0) for k in range(nl)]
    metas[1] = meta_of((pos + 1) % nl, high_end)
    metas[nl - 1] = meta_of((pos + nl - 1) % nl, low_end)
    metas.append(meta_of(jnp.where(low_end, nl - 1, 0), 0))

    def first_factor(side, slots):
        owns, recvs = [], []
        for meta, xs in zip(metas, slots):
            mine_part, send = expand(side, meta, xs, w14s, hd, sub)
            owns.append(mine_part)
            recvs.append(swap(send, n))
        return owns, recvs

    x_slots, g_slots = slots_of(x_ups, x_downs), slots_of(g_ups, g_downs)
    owns, recvs = first_factor(0, x_slots)
    z_own, z_send, *saved = middle(False, metas[0], owns, recvs, w2, w3, [], dp, scale)
    z_recv = swap(z_send, n)
    places = ((pos + jnp.arange(nl)) % nl).astype(jnp.int32)
    outs = output_parts(places, z_own, z_recv, w14s, sub)
    layer_out = lax.psum_scatter(outs, "tensor", axis_index_groups=lines).T

    owns, recvs = first_factor(1, g_slots)
    dy_own, dy_send, *g23 = middle(True, metas[0], owns, recvs, w2, w3, saved, dp, scale)
    dy_recv = swap(dy_send, n)
    parts, grads = [None] * nl, None
    order = [k for pair in zip(range(nl - 1, nl // 2, -1), range(1, nl // 2)) for k in pair]
    for k in order + [nl // 2, 0]:
        late = k in (1, nl - 1)
        xs, gs = x_slots[k], g_slots[k]
        if late:
            xs = xs + [x_slots[nl][0 if k == 1 else 1]]
            gs = gs + [g_slots[nl][0 if k == 1 else 1]]
        parts[k], *grads = contract(
            k,
            metas[k],
            (z_own, z_recv, dy_own, dy_recv),
            w14s,
            xs,
            gs,
            late,
            grads,
            sub,
            dp,
            scale,
        )

    g1, g2, g3, g4 = reduce_dp(
        [grads[:2], g23[:2], g23[2:], grads[2:]], dp, (x_first, x_first, y_first, y_first)
    )
    g14 = jnp.stack([g1, g4], axis=1)
    g14 = lax.all_to_all(
        g14, "tensor", split_axis=0, concat_axis=0, axis_index_groups=lines, tiled=True
    )

    up, down = parts[nl - 1], parts[1]
    for r in range(1, nl):
        if r == nl - 1:
            up, down, g14 = lax.optimization_barrier((up, down, g14))
        up = lax.ppermute(up, "tensor", up_pairs(0, r))
        down = lax.ppermute(down, "tensor", down_pairs(nl - 1 - r, nl - 1))
        if r < nl - 1:
            up = add(up, parts[nl - 1 - r])
            down = add(down, parts[r + 1])
            up, down = lax.optimization_barrier((up, down))

    g2 = gather_dp(g2, dp, True)
    g3 = gather_dp(g3, dp, False)
    g1 = gather_dp(g14[:, 0], dp, True)
    g4 = gather_dp(g14[:, 1], dp, False)
    tokens_grad = close(parts[0], up, down)

    base = jnp.asarray(base, jnp.int32)[None]
    offset = jnp.arange(2 * nl, dtype=jnp.int32)
    wide_rows = (((offset // 2 + pos) % nl) * 2 + (offset + core) % 2) * part
    dual_rows = (jnp.arange(dp, dtype=jnp.int32) * step + core * m) % m2
    wide_tab = jnp.concatenate([base, wide_rows.astype(jnp.int32)])
    dual_tab = jnp.concatenate([base, dual_rows.astype(jnp.int32)])
    out_two = finish(wide_tab, [g[None] for g in g2], False)
    out_three = finish(wide_tab, [g[None] for g in g3], True)
    g1, g4, out_two, out_three = lax.optimization_barrier((g1, g4, out_two, out_three))
    return (
        layer_out,
        tokens_grad,
        finish(dual_tab, g1, True),
        out_two,
        out_three,
        finish(dual_tab, g4, False),
    )


def solution(mesh):
    return jax.shard_map(
        body,
        mesh=mesh,
        in_specs=(
            P("dp", "tensor"),
            P("dp", "tensor"),
            P("tensor", None, None),
            P("tensor", None, None),
            P("tensor", None, None),
            P("tensor", None, None),
        ),
        out_specs=(
            P("dp", "tensor"),
            P("dp", "tensor"),
            P("tensor", None, None),
            P("tensor", None, None),
            P("tensor", None, None),
            P("tensor", None, None),
        ),
        check_vma=False,
    )
```
